32 devices in a mesh: sys: 2 (over y), row: 2 (over x), col: 4 (over z), aux: 2 (over core).
Axes of the slice: x: 2, y: 2, z: 4, core: 2. Of those that a mesh axis runs over, the one named last changes fastest.
Arguments:
- coef_three: bfloat16 [4, 4, 512, 16384], P(('sys', 'row'), 'col', 'aux'), parts along dimension 0, may hold values from -6 to 6
- orbitals: bfloat16 [4, 4, 40, 128], P(('sys', 'row'), 'col'), parts along dimension 0, may hold values from -0.5 to 0.5
- density: bfloat16 [4, 4, 128, 128], P(('sys', 'row'), 'col'), parts along dimension 0, may hold values from -0.5 to 0.5
- pair_mask: int32 [4, 4, 8], P(('sys', 'row'), 'col'), parts along dimension 0, may hold values 0 or 1
Outputs:
- exch_self: float32 [4, 4, 128, 128], P(('sys', 'row'), 'col', 'aux'), parts along dimension 0
- exch_pair: float32 [4, 4, 8, 128, 128], P(('sys', 'row'), 'col', None, 'aux'), parts along dimension 0
- exch_full: float32 [4, 4, 128, 128], P(('sys', 'row'), 'col', 'aux'), parts along dimension 0
The draws below stay inside these ranges and needn't reach their ends.
There are 2 independent parts, one for each index of `sys`. The reference program is written for one: setup_inputs(seed, part) draws one part's arguments, and reference() takes and returns one part's arrays. A program takes and returns all parts, laid end to end along the dimension named above; each array names one. Nothing has to cross between parts.
Inputs may be any that keep to these rules, and one draw needn't show every extreme that they name: `pair_mask`: entries for neighbours outside the grid are drawn like the others and have no effect.
All inputs are finite; a program needn't handle non-finite values. No bound on the sum of `pair_mask` on one device may be relied on, other than what follows from the above.
Results may differ from the reference program's by a relative error of at most 0.0041.
Values may be sent and summed in bfloat16 or wider, within the bound.
No kernel may reach another device: no remote copies, remote signals or barrier semaphores. Data moves between devices by JAX's collectives and lax.ppermute only.
A program may use at most 192 MiB of HBM per device.

```python
import jax
import jax.numpy as jnp
from jax import lax

NB = 128
Q = 512
OCC = 40
FROWS = 2
FCOLS = 4


def plant(array, key, smallest, top_value):
    spot = [jax.random.randint(jax.random.fold_in(key, axis), (), 0, length) for axis, length in enumerate(array.shape)]
    widest = array.shape.index(max(array.shape))
    beside = spot[:widest] + [(spot[widest] + 1) % array.shape[widest]] + spot[widest + 1:]
    return array.at[tuple(spot)].set(smallest).at[tuple(beside)].set(top_value)


def steps_of(stream_key, shape, cuts, smallest, high):
    def one(axis_at, shards_of):
        draws = jax.random.uniform(jax.random.fold_in(jax.random.fold_in(stream_key, 6), axis_at), (shards_of,), jnp.float32, smallest / len(cuts), high / len(cuts))
        return jnp.repeat(jnp.exp(draws), shape[axis_at] // shards_of).reshape((-1,) + (1,) * (len(shape) - axis_at - 1))

    loudness = one(*cuts[0])
    for cut in cuts[1:]:
        loudness = loudness * one(*cut)
    return loudness


def centred(own_key, dims, deviation, reach, shards=(), kind=jnp.bfloat16):
    array = deviation * jax.random.normal(own_key, dims, jnp.float32)
    if shards:
        array = array * steps_of(own_key, dims, shards, -0.22, 0.18)
    return jnp.clip(array, -reach, reach).astype(kind)


def setup_inputs(seed: int = 0, part: int = 0) -> dict:
    key_of = jax.random.split(jax.random.key(seed), 5)
    own_keys = jax.random.split(jax.random.fold_in(key_of[4], part), 5)
    return {
        "coef_three": centred(own_keys[0], (FROWS, FCOLS, Q, NB * NB), 1.0, 6.0, ((0, 2), (1, 4), (2, 2))),
        "orbitals": centred(own_keys[1], (FROWS, FCOLS, OCC, NB), NB ** -0.5, 0.5, ((0, 2), (1, 4))),
        "density": centred(own_keys[2], (FROWS, FCOLS, NB, NB), NB ** -0.5, 0.5, ((0, 2), (1, 4))),
        "pair_mask": plant((jax.random.randint(own_keys[3], (FROWS, FCOLS, 8), 0, 4) < 3).astype(jnp.int32), jax.random.fold_in(own_keys[3], 1), 0, 1),
    }


OFFSETS = ((-1, -1), (-1, 0), (-1, 1), (0, -1), (0, 1), (1, -1), (1, 0), (1, 1))


def contract(left, right):
    return lax.dot_general(left, right, (((0,), (0,)), ((), ())), preferred_element_type=jnp.float32)


def reference(coef_three, orbitals, density, pair_mask):
    count = FROWS * FCOLS
    flat_coef = coef_three.reshape(count, Q * NB, NB)
    flat_orb = orbitals.reshape(count, OCC, NB)
    flat_dens = density.reshape(count, NB, NB)

    def transform(pieces):
        coef, orb = pieces
        value = lax.dot_general(orb, coef, (((1,), (1,)), ((), ())), preferred_element_type=jnp.float32)
        return value.astype(jnp.bfloat16).reshape(OCC * Q, NB)

    def with_density(pieces):
        coef, dens = pieces
        dens_half = jnp.dot(coef, dens, preferred_element_type=jnp.float32).astype(jnp.bfloat16)
        left = dens_half.reshape(Q, NB, NB)
        right = coef.reshape(Q, NB, NB)
        return lax.dot_general(left, right, (((0, 2), (0, 1)), ((), ())), preferred_element_type=jnp.float32)

    half = lax.map(transform, (flat_coef, flat_orb))
    full_all = lax.map(with_density, (flat_coef, flat_dens))
    grid = half.reshape(FROWS, FCOLS, OCC * Q, NB)
    padded = jnp.pad(grid, ((1, 1), (1, 1), (0, 0), (0, 0)))
    self_scale = 1.0 / (Q * OCC)
    pair_scale = 1.0 / ((Q * OCC) ** 0.5)
    full_scale = 1.0 / ((Q * NB) ** 0.5)

    def blocks(index):
        rowpos = (index // FCOLS).astype(jnp.int32)
        colpos = (index % FCOLS).astype(jnp.int32)
        zero = jnp.zeros((), jnp.int32)
        mine = lax.dynamic_slice(padded, (rowpos + 1, colpos + 1, zero, zero), (1, 1, OCC * Q, NB))[0, 0]
        own = contract(mine, mine) * self_scale
        terms = []
        for offset in OFFSETS:
            other = lax.dynamic_slice(padded, (rowpos + 1 + offset[0], colpos + 1 + offset[1], zero, zero), (1, 1, OCC * Q, NB))[0, 0]
            terms.append(contract(mine, other))
        return own, jnp.stack(terms) * pair_scale

    own_all, pair_all = lax.map(blocks, jnp.arange(count, dtype=jnp.int32))
    exch_self = own_all.reshape(FROWS, FCOLS, NB, NB)
    maskf = pair_mask.astype(jnp.float32)
    exch_pair = pair_all.reshape(FROWS, FCOLS, 8, NB, NB) * maskf[:, :, :, None, None]
    exch_full = (full_all * full_scale).reshape(FROWS, FCOLS, NB, NB)
    return exch_self, exch_pair, exch_full
```

```python
import functools

import jax
import jax.numpy as jnp
from jax import lax
from jax.experimental import pallas as pl
from jax.experimental.pallas import tpu as pltpu
from jax.sharding import PartitionSpec as P

LANES = 128
NT = (((1,), (1,)), ((), ()))


def half_kernel(group, coef_ref, orb_ref, *refs):
    outs, scratch = refs[:-1], refs[-1]
    occupied, basis = orb_ref.shape
    slabs, _, lanes = scratch.shape
    pitch = scratch.shape[1] // group
    orb = orb_ref[...]
    for j in range(group):
        value = lax.dot_general(
            orb, coef_ref[:, j * basis : (j + 1) * basis], NT, preferred_element_type=jnp.float32
        )
        for h in range(slabs):
            scratch[h, j * pitch : j * pitch + occupied, :] = value[:, h * lanes : (h + 1) * lanes]
    o = 0
    for out in outs:
        for i in range(out.shape[1] // (slabs * lanes)):
            for h in range(slabs):
                at = (i * slabs + h) * lanes
                out[:, at : at + lanes] = scratch[h, pl.ds(o, group, stride=pitch), :].astype(out.dtype)
            o += 1


def half_call(coef, orb, counts, group=32):
    q, width = coef.shape
    occupied, basis = orb.shape
    pitch = occupied + 8 * (1 - (occupied // 8) % 2)
    return pl.pallas_call(
        functools.partial(half_kernel, group),
        grid=(basis // group,),
        in_specs=[
            pl.BlockSpec((q, group * basis), lambda i: (0, i)),
            pl.BlockSpec((occupied, basis), lambda i: (0, 0)),
        ],
        out_specs=[pl.BlockSpec((group, n * q), lambda i: (i, 0)) for n in counts],
        out_shape=[jax.ShapeDtypeStruct((basis, n * q), jnp.bfloat16) for n in counts],
        scratch_shapes=[pltpu.VMEM((q // LANES, group * pitch, LANES), jnp.float32)],
        cost_estimate=pl.CostEstimate(
            flops=2 * q * width * occupied,
            bytes_accessed=2 * q * width + 2 * occupied * basis * q,
            transcendentals=0,
        ),
        name="half",
    )(coef, orb)


def full_kernel(group, coef_ref, dens_ref, out_ref, kept, turned, scratch, total):
    basis = dens_ref.shape[0]
    slabs, rows, lanes = scratch.shape
    pitch = rows // group
    i = pl.program_id(0)
    dens = dens_ref[...]
    for j in range(group):
        value = lax.dot_general(
            dens,
            coef_ref[:, j * basis : (j + 1) * basis],
            (((0,), (1,)), ((), ())),
            preferred_element_type=jnp.float32,
        )
        for h in range(slabs):
            scratch[h, j * pitch : j * pitch + basis, :] = value[:, h * lanes : (h + 1) * lanes]
    kept[:, pl.ds(pl.multiple_of(i * group * basis, group * basis), group * basis)] = coef_ref[...]

    @pl.loop(0, basis, unroll=8)
    def _(s):
        for h in range(slabs):
            turned[s, pl.ds(pl.multiple_of(i * group, group), group), h * lanes : (h + 1) * lanes] = scratch[
                h, pl.ds(s, group, stride=pitch), :
            ].astype(turned.dtype)

    @pl.when(i == pl.num_programs(0) - 1)
    def _():
        total[...] = jnp.zeros_like(total)

        @pl.loop(0, basis, step=8)
        def _(first):
            part = jnp.zeros(total.shape, jnp.float32)
            for k in range(8):
                s = first + k
                part += jnp.dot(
                    turned[s],
                    kept[:, pl.ds(pl.multiple_of(s * basis, basis), basis)],
                    preferred_element_type=jnp.float32,
                )
            total[...] += part

        out_ref[...] = total[...]


def full_call(coef, dens, group=32):
    q, width = coef.shape
    basis = dens.shape[0]
    pitch = basis + 8
    return pl.pallas_call(
        functools.partial(full_kernel, group),
        grid=(basis // group,),
        in_specs=[
            pl.BlockSpec((q, group * basis), lambda i: (0, i)),
            pl.BlockSpec((basis, basis), lambda i: (0, 0)),
        ],
        out_specs=pl.BlockSpec((basis, basis), lambda i: (0, 0)),
        out_shape=jax.ShapeDtypeStruct((basis, basis), jnp.float32),
        scratch_shapes=[
            pltpu.VMEM((q, width), jnp.bfloat16),
            pltpu.VMEM((basis, basis, q), jnp.bfloat16),
            pltpu.VMEM((q // LANES, group * pitch, LANES), jnp.float32),
            pltpu.VMEM((basis, basis), jnp.float32),
        ],
        compiler_params=pltpu.CompilerParams(vmem_limit_bytes=40 * 2**20),
        cost_estimate=pl.CostEstimate(
            flops=4 * q * width * basis, bytes_accessed=2 * q * width, transcendentals=0
        ),
        name="full",
    )(coef, dens)


def gram(left, right):
    return lax.dot_general(left, right, NT, preferred_element_type=jnp.float32)


def row_pairs(rows, shift):
    first = [(i, i + 1) for i in range(shift, rows - 1, 2)]
    return first + [(j, i) for i, j in first]


def along(value, step):
    count = lax.axis_size("col")
    first, last = max(0, -step), min(count, count - step)
    return lax.ppermute(value, "col", [(i, i + step) for i in range(first, last)])


def over_aux(stack):
    side = lax.axis_index("aux")
    half = stack.shape[1] // 2
    mine = lax.dynamic_slice_in_dim(stack, side * half, half, 1)
    theirs = lax.dynamic_slice_in_dim(stack, (1 - side) * half, half, 1)
    return mine + lax.ppermute(theirs, "aux", [(0, 1), (1, 0)])


def chunked(count):
    small = max(1, count // 5)
    big = (count - small) // 2
    return [count - small - big, big, small]


def local(coef_three, orbitals, density, pair_mask, *, full_q):
    _, _, q, width = coef_three.shape
    occupied, basis = orbitals.shape[2:]
    rows = lax.axis_size("row")
    coef = coef_three.reshape(q, width)
    orb = orbitals[0, 0]
    odd = lax.axis_index("row") % 2
    kept_count = occupied // 2
    quarter = kept_count // 2
    ordered = jnp.concatenate(
        [
            lax.dynamic_slice_in_dim(orb, odd * kept_count, kept_count, 0),
            lax.dynamic_slice_in_dim(orb, (1 - odd) * kept_count, kept_count, 0),
        ]
    )
    sizes = chunked(quarter)
    steps = len(sizes)
    outs = half_call(coef, ordered, [quarter, quarter] + sizes + sizes)
    keep_w, keep_e = outs[:2]
    send_w, send_e = outs[2 : 2 + steps], outs[2 + steps :]
    edges = [0]
    for n in sizes:
        edges.append(edges[-1] + n * q)

    def cut(value, k):
        return value[:, edges[k] : edges[k + 1]]

    west = along(keep_w, -1)
    east = along(keep_e, 1)
    own = gram(keep_w, keep_w) + gram(keep_e, keep_e)
    for piece in list(send_w) + list(send_e):
        own += gram(piece, piece)
    xx_r = gram(keep_w, west)
    xx_l = gram(keep_e, east)
    passes = []
    for shift in range(min(2, rows - 1)):
        swap = row_pairs(rows, shift)
        upright = 0.0
        yx_r = yx_l = xy_r = xy_l = yy_r = yy_l = 0.0
        for k in range(steps):
            y_w = lax.ppermute(send_w[k], "row", swap)
            y_e = lax.ppermute(send_e[k], "row", swap)
            upright += gram(cut(keep_w, k), y_w) + gram(cut(keep_e, k), y_e)
            yx_r += gram(y_w, cut(west, k))
            yx_l += gram(y_e, cut(east, k))
            far_w = along(y_w, -1)
            far_e = along(y_e, 1)
            xy_r += gram(cut(keep_w, k), far_w)
            xy_l += gram(cut(keep_e, k), far_e)
            if shift == 0:
                yy_r += gram(y_w, far_w)
                yy_l += gram(y_e, far_e)
        passes.append((swap, upright, yx_r, yx_l, xy_r, xy_l, yy_r, yy_l))
    full = full_call(coef, density[0, 0])

    t = jnp.transpose
    side = over_aux(jnp.stack([own, full]))
    self_part, full_part = side[0], side[1]
    mask = pair_mask[0, 0].astype(jnp.float32) * (1.0 / (full_q * occupied) ** 0.5)
    zero = jnp.zeros((basis // 2, basis), jnp.float32)
    up, down = [zero] * 3, [zero] * 3
    level = [zero, zero]
    for shift, (swap, upright, yx_r, yx_l, xy_r, xy_l, yy_r, yy_l) in enumerate(passes):
        lines = over_aux(jnp.stack([upright, t(upright)]))
        out = [yx_r, yx_l, t(xy_r), t(xy_l)]
        mine = [xy_r, xy_l, t(yx_r), t(yx_l)]
        if shift == 0:
            out += [yy_r, yy_l, t(yy_r), t(yy_l)]
            mine += [xx_r, xx_l, t(xx_r), t(xx_l)]
        n = len(out)
        joined = over_aux(jnp.stack(mine + out))
        vertical = lines[0] + lax.ppermute(lines[1], "row", swap)
        joined = joined[:n] + lax.ppermute(joined[n:], "row", swap)
        onward_e = joined[2::4]
        onward_w = joined[3::4]
        from_w = along(onward_e, 1)
        from_e = along(onward_w, -1)
        three = [joined[1] + from_w[0], vertical, joined[0] + from_e[0]]
        if shift == 0:
            level = [joined[5] + from_w[1], joined[4] + from_e[1]]
        is_down = (odd == shift).astype(jnp.float32)
        up = [a + b * (1.0 - is_down) for a, b in zip(up, three)]
        down = [a + b * is_down for a, b in zip(down, three)]
    pair = jnp.stack(up + level + down) * mask[:, None, None]
    exch_self = self_part * (1.0 / (full_q * occupied))
    exch_full = full_part * (1.0 / (full_q * basis) ** 0.5)
    return exch_self[None, None], pair[None, None], exch_full[None, None]


def solution(mesh):
    in_specs = (
        P(("sys", "row"), "col", "aux", None),
        P(("sys", "row"), "col", None, None),
        P(("sys", "row"), "col", None, None),
        P(("sys", "row"), "col", None),
    )
    out_specs = (
        P(("sys", "row"), "col", "aux", None),
        P(("sys", "row"), "col", None, "aux", None),
        P(("sys", "row"), "col", "aux", None),
    )

    def whole(coef_three, orbitals, density, pair_mask):
        return jax.shard_map(
            functools.partial(local, full_q=coef_three.shape[2]),
            mesh=mesh,
            in_specs=in_specs,
            out_specs=out_specs,
            check_vma=False,
        )(coef_three, orbitals, density, pair_mask)

    return whole
```

```python
import functools

import jax
import jax.numpy as jnp
from jax import lax
from jax.experimental import pallas as pl
from jax.experimental.pallas import tpu as pltpu
from jax.sharding import PartitionSpec as P


LANES = 128
NT = (((1,), (1,)), ((), ()))
WHOLE = pl.BlockSpec(memory_space=pltpu.VMEM)
SMEM = pl.BlockSpec(memory_space=pltpu.SMEM)
F32 = jnp.float32
BF16 = jnp.bfloat16
BATCH = 2
SMALL = pltpu.CompilerParams(vmem_limit_bytes=12 * 2**20)


def cost(flops, size):
    return pl.CostEstimate(flops=int(flops), bytes_accessed=int(size), transcendentals=0)


def odd_pitch(rows):
    return rows + 8 * (1 - (rows // 8) % 2)


def slabs_of(coef_ref, first, basis):
    return jnp.concatenate([coef_ref[:, j * basis : (j + 1) * basis] for j in range(first, first + BATCH)])


def half_kernel(group, counts, coef_ref, orb_ref, *refs):
    outs, scratch = refs[:-1], refs[-1]
    occupied, basis = orb_ref.shape
    slabs, rows, lanes = scratch.shape
    pitch = rows // group
    quarter = occupied // 4
    flip_row = lax.axis_index("row") % 2
    flip_col = lax.axis_index("col") % 2
    orb = orb_ref[...]
    for j in range(0, group, BATCH):
        value = lax.dot_general(orb, slabs_of(coef_ref, j, basis), NT, preferred_element_type=F32)
        for k in range(BATCH * slabs):
            at = (j + k // slabs) * pitch
            scratch[k % slabs, at : at + occupied, :] = value[:, k * lanes : (k + 1) * lanes]
    o = 0
    for out, count in zip(outs, counts):
        for i in range(count):
            send, turn = o // (2 * quarter), o // quarter % 2
            away = flip_row if send == 0 else 1 - flip_row
            over = 1 - flip_col if turn == 0 else flip_col
            row = o % quarter + 2 * quarter * away + quarter * over
            for h in range(slabs):
                at = (i * slabs + h) * lanes
                out[:, at : at + lanes] = scratch[h, pl.ds(row, group, stride=pitch), :].astype(BF16)
            o += 1


def half_call(coef, orb, counts, group=64):
    q, width = coef.shape
    occupied, basis = orb.shape
    pitch = odd_pitch(occupied)
    return pl.pallas_call(
        functools.partial(half_kernel, group, counts),
        grid=(basis // group,),
        in_specs=[
            pl.BlockSpec((q, group * basis), lambda i: (0, i)),
            pl.BlockSpec((occupied, basis), lambda i: (0, 0)),
        ],
        out_specs=[pl.BlockSpec((group, n * q), lambda i: (i, 0)) for n in counts],
        out_shape=[jax.ShapeDtypeStruct((basis, n * q), BF16) for n in counts],
        scratch_shapes=[pltpu.VMEM((q // LANES, group * pitch, LANES), F32)],
        cost_estimate=cost(2 * q * width * occupied, 2 * q * width + 2 * occupied * basis * q),
        name="half",
    )(coef, orb)


def full_kernel(group, coef_ref, dens_ref, mine, theirs, kept, turned, scratch, total):
    basis = dens_ref.shape[0]
    slabs, rows, lanes = scratch.shape
    q = slabs * lanes
    pitch = rows // group
    i = pl.program_id(0)
    at = pl.ds(pl.multiple_of(i * group, group), group)
    dens = dens_ref[...].T
    for j in range(0, group, BATCH):
        slab = slabs_of(coef_ref, j, basis)
        kept[pl.ds(pl.multiple_of((i * group + j) * q, q), BATCH * q), :] = slab
        value = lax.dot_general(dens, slab, NT, preferred_element_type=F32)
        for k in range(BATCH * slabs):
            to = (j + k // slabs) * pitch
            scratch[k % slabs, to : to + basis, :] = value[:, k * lanes : (k + 1) * lanes]
    for s in range(basis):
        for h in range(slabs):
            turned[at, s * q + h * lanes : s * q + (h + 1) * lanes] = scratch[
                h, pl.ds(s, group, stride=pitch), :
            ].astype(BF16)

    @pl.when(i == pl.num_programs(0) - 1)
    def _():
        total[...] = jnp.zeros_like(total)
        span = basis // 4 * q

        @pl.loop(0, basis * q, step=span)
        def _(first):
            here = pl.ds(pl.multiple_of(first, span), span)
            total[...] += jnp.dot(turned[:, here], kept[here, :], preferred_element_type=F32)

        half = basis // 2
        side = lax.axis_index("aux")
        mine[...] = total[pl.ds(pl.multiple_of(side * half, half), half), :]
        theirs[...] = total[pl.ds(pl.multiple_of((1 - side) * half, half), half), :]


def full_call(coef, dens, group=32):
    q, width = coef.shape
    basis = dens.shape[0]
    pitch = odd_pitch(basis)
    half = jax.ShapeDtypeStruct((basis // 2, basis), F32)
    return pl.pallas_call(
        functools.partial(full_kernel, group),
        grid=(basis // group,),
        in_specs=[
            pl.BlockSpec((q, group * basis), lambda i: (0, i)),
            pl.BlockSpec((basis, basis), lambda i: (0, 0)),
        ],
        out_specs=[pl.BlockSpec((basis // 2, basis), lambda i: (0, 0))] * 2,
        out_shape=[half, half],
        scratch_shapes=[
            pltpu.VMEM((q * basis, basis), BF16),
            pltpu.VMEM((basis, basis * q), BF16),
            pltpu.VMEM((q // LANES, group * pitch, LANES), F32),
            pltpu.VMEM((basis, basis), F32),
        ],
        cost_estimate=cost(4 * q * width * basis, 2 * q * width),
        name="full",
    )(coef, dens)


def nt(left, right):
    return lax.dot_general(left, right, NT, preferred_element_type=F32)


def meet(x_e, x_o, far_e, far_o, y_e, y_o, farther_e, farther_o):
    near_e = jnp.concatenate([x_e[...], y_e[...]])
    near_o = jnp.concatenate([x_o[...], y_o[...]])
    even = nt(near_o, jnp.concatenate([far_e[...], farther_e[...]]))
    odd = nt(near_e, jnp.concatenate([far_o[...], farther_o[...]]))
    return even, odd, nt(near_e, near_e) + nt(near_o, near_o)


def meet_kernel(*refs):
    before, outs = refs[8:-3], refs[-3:]
    for k, value in enumerate(meet(*refs[:8])):
        outs[k][...] = value + before[k][...] if before else value


def last_kernel(*refs):
    before, (mine, theirs, lines) = refs[8:-3], refs[-3:]
    basis = mine.shape[2] // 2
    half = basis // 2
    sums = list(meet(*refs[:8]))
    for k, part in enumerate(before):
        sums[k] += part[...]
    for k in range(3):
        lines[k] = sums[k][:basis]
        lines[3 + k] = sums[k][basis:]
    for k in range(2):
        turned = sums[k].T
        lines[6 + 2 * k] = turned[:basis]
        lines[7 + 2 * k] = turned[basis:]
    side = lax.axis_index("aux")
    mine[...] = lines[:, pl.ds(pl.multiple_of(side * half, half), half), :]
    theirs[...] = lines[:, pl.ds(pl.multiple_of((1 - side) * half, half), half), :]


def meet_call(block, xs, ys, before, last):
    basis, width = ys[0].shape
    two = jax.ShapeDtypeStruct((2 * basis, 2 * basis), F32)
    out = jax.ShapeDtypeStruct((10, basis // 2, 2 * basis), F32)
    return pl.pallas_call(
        last_kernel if last else meet_kernel,
        grid=(1,),
        in_specs=[pl.BlockSpec((basis, width), lambda i: (0, block))] * 4
        + [pl.BlockSpec((basis, width), lambda i: (0, 0))] * 4
        + [pl.BlockSpec(two.shape, lambda i: (0, 0))] * len(before),
        out_specs=[pl.BlockSpec(out.shape, lambda i: (0, 0, 0))] * 2
        if last
        else [pl.BlockSpec(two.shape, lambda i: (0, 0))] * 3,
        out_shape=[out, out] if last else [two, two, two],
        scratch_shapes=[pltpu.VMEM((10, basis, 2 * basis), F32)] if last else [],
        cost_estimate=cost(24 * basis * basis * width, 16 * basis * width),
        compiler_params=SMALL,
    )(*xs, *ys, *before)


def joined_kernel(mine, theirs, stay, even, odd):
    stay[...] = mine[0:6] + theirs[0:6]
    even[...] = (mine[6:8] + theirs[6:8]).astype(BF16)
    odd[...] = (mine[8:10] + theirs[8:10]).astype(BF16)


def joined_call(mine, theirs):
    _, half, two = mine.shape
    onward = jax.ShapeDtypeStruct((2, half, two), BF16)
    return pl.pallas_call(
        joined_kernel,
        in_specs=[WHOLE] * 2,
        out_specs=[WHOLE] * 3,
        out_shape=[jax.ShapeDtypeStruct((6, half, two), F32), onward, onward],
        cost_estimate=cost(mine.size, 12 * mine.size),
        compiler_params=SMALL,
        name="joined",
    )(mine, theirs)


def across_kernel(stay, even, odd, keep, send):
    keep[0] = stay[0] + even[0].astype(F32)
    keep[1] = stay[1] + odd[0].astype(F32)
    keep[2] = stay[2]
    send[0] = (stay[3] + even[1].astype(F32)).astype(BF16)
    send[1] = (stay[4] + odd[1].astype(F32)).astype(BF16)
    send[2] = stay[5].astype(BF16)


def across_call(stay, even, odd):
    _, half, two = stay.shape
    return pl.pallas_call(
        across_kernel,
        in_specs=[WHOLE] * 3,
        out_specs=[WHOLE] * 2,
        out_shape=[jax.ShapeDtypeStruct((3, half, two), F32), jax.ShapeDtypeStruct((3, half, two), BF16)],
        cost_estimate=cost(stay.size, 8 * stay.size),
        compiler_params=SMALL,
        name="across",
    )(stay, even, odd)


def finish_kernel(scales, mask, full_mine, full_theirs, *refs):
    self_scale, pair_scale, full_scale = scales
    ins, (self_out, pair_out, full_out) = refs[:-3], refs[-3:]
    basis = self_out.shape[1]
    row, col = lax.axis_index("row"), lax.axis_index("col")
    rows, cols = lax.axis_size("row"), lax.axis_size("col")
    even_right = 1 - col % 2

    def put(down, right, value):
        d = (down + 1) * 3 + right + 1
        d = d - (d > 4).astype(jnp.int32)
        r, c = row + down, col + right
        inside = (r >= 0) & (r < rows) & (c >= 0) & (c < cols)
        factor = jnp.where(inside, mask[0, d].astype(F32) * pair_scale, 0.0)
        pair_out[d] = value * factor

    to_even, to_odd = 2 * even_right - 1, 1 - 2 * even_right
    full_out[...] = (full_mine[...] + full_theirs[...]) * full_scale
    if len(ins) == 2:
        for d in range(3):
            pair_out[jnp.where(row % 2 == 0, d, 5 + d)] = jnp.zeros_like(full_mine)
    for shift in range(len(ins) // 2):
        keep, got = ins[2 * shift : 2 * shift + 2]
        down = 2 * (row % 2 == shift).astype(jnp.int32) - 1
        own = [keep[k, :, :basis] + got[k, :, basis:].astype(F32) for k in range(3)]
        other = [keep[k, :, basis:] + got[k, :, :basis].astype(F32) for k in range(3)]
        put(down, to_even, other[0])
        put(down, to_odd, other[1])
        put(down, 0, other[2])
        if shift == 0:
            put(0, to_even, own[0])
            put(0, to_odd, own[1])
            self_out[...] = own[2] * self_scale


def finish_call(mask, full, results, scales):
    args = [*full, *(a for result in results for a in result)]
    half, basis = full[0].shape
    side = jax.ShapeDtypeStruct((half, basis), F32)
    return pl.pallas_call(
        functools.partial(finish_kernel, scales),
        in_specs=[SMEM] + [WHOLE] * len(args),
        out_specs=[WHOLE] * 3,
        out_shape=[side, jax.ShapeDtypeStruct((8, half, basis), F32), side],
        cost_estimate=cost(20 * half * basis, 80 * half * basis),
        compiler_params=SMALL,
        name="finish",
    )(mask, *args)


def row_pairs(rows, shift):
    first = [(i, i + 1) for i in range(shift, rows - 1, 2)]
    return first + [(j, i) for i, j in first]


def beside(value, first):
    cols, sides = lax.axis_size("col"), lax.axis_size("aux")
    pairs = []
    for c in range(cols):
        other = c ^ 1 if first == 0 else ((c - 1) ^ 1) + 1
        for a in range(sides):
            inside = 0 <= other < cols
            pairs.append((c * sides + a, other * sides + a if inside else c * sides + (a + 1) % sides))
    return lax.ppermute(value, ("col", "aux"), pairs)


def chunks(quarter):
    if quarter % 5 == 0:
        return [2 * quarter // 5, 2 * quarter // 5, quarter // 5]
    return [quarter // 2] * 2 if quarter % 2 == 0 else [quarter]


def local(coef_three, orbitals, density, pair_mask, *, full_q):
    _, _, q, width = coef_three.shape
    occupied, basis = orbitals.shape[2:]
    rows = lax.axis_size("row")
    coef = coef_three.reshape(q, width)
    quarter = occupied // 4
    sizes = chunks(quarter)
    steps = len(sizes)
    outs = half_call(coef, orbitals[0, 0], [quarter] * 2 + sizes * 2)
    keep_e, keep_o = outs[:2]
    sends = list(zip(outs[2 : 2 + steps], outs[2 + steps :]))
    swap_sides = [(0, 1), (1, 0)]
    full_mine, full_theirs = full_call(coef, density[0, 0])
    full = (full_mine, lax.ppermute(full_theirs, "aux", swap_sides))
    near = (keep_e, keep_o, beside(keep_e, 0), beside(keep_o, 1))
    results = []
    for shift in range(min(2, rows - 1)):
        swap = row_pairs(rows, shift)
        sums, start = (), 0
        pieces = []
        for send_e, send_o in sends:
            y_e = lax.ppermute(send_e, "row", swap)
            y_o = lax.ppermute(send_o, "row", swap)
            pieces.append((y_e, y_o, beside(y_e, 0), beside(y_o, 1)))
        for k, piece in enumerate(pieces):
            last = k == steps - 1
            sums = meet_call(start // sizes[k], near, piece, sums, last)
            start += sizes[k]
        mine, theirs = sums
        stay, even, odd = joined_call(mine, lax.ppermute(theirs, "aux", swap_sides))
        keep, send = across_call(stay, beside(even, 0), beside(odd, 1))
        results.append((keep, lax.ppermute(send, "row", swap)))
    scales = (
        1.0 / (full_q * occupied),
        1.0 / (full_q * occupied) ** 0.5,
        1.0 / (full_q * basis) ** 0.5,
    )
    exch_self, pair, exch_full = finish_call(pair_mask[0], full, results, scales)
    return exch_self[None, None], pair[None, None], exch_full[None, None]


def solution(mesh):
    in_specs = (
        P(("sys", "row"), "col", "aux", None),
        P(("sys", "row"), "col", None, None),
        P(("sys", "row"), "col", None, None),
        P(("sys", "row"), "col", None),
    )
    out_specs = (
        P(("sys", "row"), "col", "aux", None),
        P(("sys", "row"), "col", None, "aux", None),
        P(("sys", "row"), "col", "aux", None),
    )

    def whole(coef_three, orbitals, density, pair_mask):
        return jax.shard_map(
            functools.partial(local, full_q=coef_three.shape[2]),
            mesh=mesh,
            in_specs=in_specs,
            out_specs=out_specs,
            check_vma=False,
        )(coef_three, orbitals, density, pair_mask)

    return whole
```

```python
import functools

import jax
import jax.numpy as jnp
from jax import lax
from jax.experimental import pallas as pl
from jax.experimental.pallas import tpu as pltpu
from jax.sharding import PartitionSpec as P


LANES = 128
NT = (((1,), (1,)), ((), ()))
HBM = pl.BlockSpec(memory_space=pltpu.HBM)
WHOLE = pl.BlockSpec(memory_space=pltpu.VMEM)
SMEM = pl.BlockSpec(memory_space=pltpu.SMEM)
F32 = jnp.float32
BF16 = jnp.bfloat16
BATCH = 4
MIB = 2**20
SMALL = pltpu.CompilerParams(vmem_limit_bytes=12 * MIB)


def cost(flops, size):
    return pl.CostEstimate(flops=int(flops), bytes_accessed=int(size), transcendentals=0)


def odd_pitch(rows):
    return rows + 8 * (1 - (rows // 8) % 2)


def block(i, size):
    return pl.ds(pl.multiple_of(i * size, size), size)


def put_slabs(scratch, group, left, kept, i):
    height, (slabs, rows, lanes) = left.shape[0], scratch.shape
    pitch, q = rows // group, slabs * lanes
    for j in range(0, group, BATCH):
        first = pl.multiple_of((i * group + j) * q, BATCH * q)
        value = nt(left, kept[pl.ds(first, BATCH * q), :])
        for k in range(BATCH * slabs):
            at = (j + k // slabs) * pitch
            scratch[k % slabs, at : at + height, :] = value[:, k * lanes : (k + 1) * lanes]
    return pitch


def half_kernel(part, group, counts, coef, orb, *refs):
    outs, (kept, scratch, orb_ref, arrived) = refs[:-4], refs[-4:]
    occupied, basis = orb.shape
    slabs, _, lanes = scratch.shape
    q = slabs * lanes
    steps = basis // group
    quarter = occupied // 4
    flip_row = lax.axis_index("row") % 2
    flip_col = lax.axis_index("col") % 2
    copy = pltpu.make_async_copy(orb, orb_ref, arrived.at[steps])
    copy.start()

    @pl.loop(0, steps)
    def _(i):
        for j in range(group):
            k = i * group + j
            pltpu.make_async_copy(
                coef.at[part * q : (part + 1) * q, block(k, basis)], kept.at[block(k, q), :], arrived.at[i]
            ).start()

    copy.wait()
    orb = orb_ref[...]

    @pl.loop(0, steps)
    def _(i):
        here = kept.at[block(i, group * q), :]
        pltpu.make_async_copy(here, here, arrived.at[i]).wait()
        pitch = put_slabs(scratch, group, orb, kept, i)
        o = 0
        for out, count in zip(outs, counts):
            for k in range(count):
                send, turn = o // (2 * quarter), o // quarter % 2
                away = flip_row if send == 0 else 1 - flip_row
                over = 1 - flip_col if turn == 0 else flip_col
                row = o % quarter + 2 * quarter * away + quarter * over
                for h in range(slabs):
                    at = (k * slabs + h) * lanes
                    out[block(i, group), at : at + lanes] = scratch[h, pl.ds(row, group, stride=pitch), :].astype(BF16)
                o += 1


def half_call(coef, orb, part, parts, counts, grant, group=32):
    q, width = coef.shape
    q //= parts
    occupied, basis = orb.shape
    shapes = [(basis, n * q) for n in counts] + [(basis * q, basis)]
    return pl.pallas_call(
        functools.partial(half_kernel, part, group, counts),
        in_specs=[HBM, HBM],
        out_specs=[WHOLE] * len(shapes),
        out_shape=[jax.ShapeDtypeStruct(shape, BF16) for shape in shapes],
        scratch_shapes=[
            pltpu.VMEM((q // LANES, group * odd_pitch(occupied), LANES), F32),
            pltpu.VMEM(orb.shape, BF16),
            pltpu.SemaphoreType.DMA((basis // group + 1,)),
        ],
        cost_estimate=cost(2 * q * width * occupied, 2 * q * width + 2 * occupied * basis * q),
        compiler_params=pltpu.CompilerParams(vmem_limit_bytes=grant * MIB),
    )(coef, orb)


def full_kernel(group, kept, dens_ref, *refs):
    before, outs, (turned, scratch) = refs[:-4], refs[-4:-2], refs[-2:]
    basis = dens_ref.shape[0]
    slabs, _, lanes = scratch.shape
    q = slabs * lanes
    dens = dens_ref[...].T

    @pl.loop(0, basis // group)
    def _(i):
        pitch = put_slabs(scratch, group, dens, kept, i)
        for s in range(basis):
            for h in range(slabs):
                at = s * q + h * lanes
                turned[block(i, group), at : at + lanes] = scratch[h, pl.ds(s, group, stride=pitch), :].astype(BF16)

    total = before[0][...] + before[1][...] if before else jnp.zeros((basis, basis), F32)
    span = basis // 2 * q
    for first in range(0, basis * q, span):
        total += jnp.dot(turned[:, first : first + span], kept[first : first + span, :], preferred_element_type=F32)
    half = basis // 2
    side = lax.axis_index("aux")
    if before:
        scratch[0, :basis, :] = total
        outs[0][...] = scratch[0, block(side, half), :]
        outs[1][...] = scratch[0, block(1 - side, half), :]
    else:
        outs[0][...] = total
        outs[1][...] = jnp.zeros_like(outs[1])


def full_call(kept, dens, before, group=64):
    basis = dens.shape[0]
    q = kept.shape[0] // basis
    height = basis // 2 if before else basis
    out = jax.ShapeDtypeStruct((height, basis), F32)
    args = [kept, dens, *before]
    return pl.pallas_call(
        functools.partial(full_kernel, group),
        in_specs=[WHOLE] * len(args),
        out_specs=[WHOLE] * 2,
        out_shape=[out, out],
        scratch_shapes=[
            pltpu.VMEM((basis, basis * q), BF16),
            pltpu.VMEM((q // LANES, group * odd_pitch(basis), LANES), F32),
        ],
        compiler_params=pltpu.CompilerParams(vmem_limit_bytes=16 * MIB),
        cost_estimate=cost(4 * q * basis**3, 2 * q * basis**2),
    )(*args)


def nt(left, right):
    return lax.dot_general(left, right, NT, preferred_element_type=F32)


def meet(start, x_e, x_o, far_e, far_o, y_e, y_o, farther_e, farther_o):
    here = slice(start, start + y_e.shape[1])
    near_e = jnp.concatenate([x_e[:, here], y_e[...]])
    near_o = jnp.concatenate([x_o[:, here], y_o[...]])
    even = nt(near_o, jnp.concatenate([far_e[:, here], farther_e[...]]))
    odd = nt(near_e, jnp.concatenate([far_o[:, here], farther_o[...]]))
    return even, odd, nt(near_e, near_e) + nt(near_o, near_o)


def meet_kernel(start, *refs):
    before, outs = refs[8:-3], refs[-3:]
    for k, value in enumerate(meet(start, *refs[:8])):
        outs[k][...] = value + before[k][...] if before else value


def last_kernel(start, *refs):
    before, (mine, theirs, lines) = refs[8:-3], refs[-3:]
    basis = mine.shape[2] // 2
    half = basis // 2
    sums = list(meet(start, *refs[:8]))
    for k, part in enumerate(before):
        sums[k] += part[...]
    for k in range(3):
        lines[k] = sums[k][:basis]
        lines[3 + k] = sums[k][basis:]
    for k in range(2):
        turned = sums[k].T
        lines[6 + 2 * k] = turned[:basis]
        lines[7 + 2 * k] = turned[basis:]
    side = lax.axis_index("aux")
    mine[...] = lines[:, pl.ds(pl.multiple_of(side * half, half), half), :]
    theirs[...] = lines[:, pl.ds(pl.multiple_of((1 - side) * half, half), half), :]


def meet_call(start, xs, ys, before, last):
    basis, width = ys[0].shape
    two = jax.ShapeDtypeStruct((2 * basis, 2 * basis), F32)
    out = jax.ShapeDtypeStruct((10, basis // 2, 2 * basis), F32)
    args = [*xs, *ys, *before]
    shapes = [out, out] if last else [two, two, two]
    return pl.pallas_call(
        functools.partial(last_kernel if last else meet_kernel, start),
        in_specs=[WHOLE] * len(args),
        out_specs=[WHOLE] * len(shapes),
        out_shape=shapes,
        scratch_shapes=[pltpu.VMEM((10, basis, 2 * basis), F32)] if last else [],
        cost_estimate=cost(24 * basis * basis * width, 16 * basis * width),
        compiler_params=SMALL,
    )(*args)


def joined_kernel(mine, theirs, stay, even, odd):
    stay[...] = mine[0:6] + theirs[0:6]
    even[...] = (mine[6:8] + theirs[6:8]).astype(BF16)
    odd[...] = (mine[8:10] + theirs[8:10]).astype(BF16)


def joined_call(mine, theirs):
    _, half, two = mine.shape
    onward = jax.ShapeDtypeStruct((2, half, two), BF16)
    return pl.pallas_call(
        joined_kernel,
        in_specs=[WHOLE] * 2,
        out_specs=[WHOLE] * 3,
        out_shape=[jax.ShapeDtypeStruct((6, half, two), F32), onward, onward],
        cost_estimate=cost(mine.size, 12 * mine.size),
        compiler_params=SMALL,
        name="joined",
    )(mine, theirs)


def across_kernel(stay, even, odd, keep, send):
    keep[0] = stay[0] + even[0].astype(F32)
    keep[1] = stay[1] + odd[0].astype(F32)
    keep[2] = stay[2]
    send[0] = (stay[3] + even[1].astype(F32)).astype(BF16)
    send[1] = (stay[4] + odd[1].astype(F32)).astype(BF16)
    send[2] = stay[5].astype(BF16)


def across_call(stay, even, odd):
    _, half, two = stay.shape
    return pl.pallas_call(
        across_kernel,
        in_specs=[WHOLE] * 3,
        out_specs=[WHOLE] * 2,
        out_shape=[jax.ShapeDtypeStruct((3, half, two), F32), jax.ShapeDtypeStruct((3, half, two), BF16)],
        cost_estimate=cost(stay.size, 8 * stay.size),
        compiler_params=SMALL,
        name="across",
    )(stay, even, odd)


def finish_kernel(scales, mask, full_mine, full_theirs, *refs):
    self_scale, pair_scale, full_scale = scales
    ins, (self_out, pair_out, full_out) = refs[:-3], refs[-3:]
    basis = self_out.shape[1]
    row, col = lax.axis_index("row"), lax.axis_index("col")
    rows, cols = lax.axis_size("row"), lax.axis_size("col")
    even_right = 1 - col % 2

    def put(down, right, value):
        d = (down + 1) * 3 + right + 1
        d = d - (d > 4).astype(jnp.int32)
        r, c = row + down, col + right
        inside = (r >= 0) & (r < rows) & (c >= 0) & (c < cols)
        factor = jnp.where(inside, mask[0, d].astype(F32) * pair_scale, 0.0)
        pair_out[d] = value * factor

    to_even, to_odd = 2 * even_right - 1, 1 - 2 * even_right
    full_out[...] = (full_mine[...] + full_theirs[...]) * full_scale
    if len(ins) == 2:
        for d in range(3):
            pair_out[jnp.where(row % 2 == 0, d, 5 + d)] = jnp.zeros_like(full_mine)
    for shift in range(len(ins) // 2):
        keep, got = ins[2 * shift : 2 * shift + 2]
        down = 2 * (row % 2 == shift).astype(jnp.int32) - 1
        own = [keep[k, :, :basis] + got[k, :, basis:].astype(F32) for k in range(3)]
        other = [keep[k, :, basis:] + got[k, :, :basis].astype(F32) for k in range(3)]
        put(down, to_even, other[0])
        put(down, to_odd, other[1])
        put(down, 0, other[2])
        if shift == 0:
            put(0, to_even, own[0])
            put(0, to_odd, own[1])
            self_out[...] = own[2] * self_scale


def finish_call(mask, full, results, scales):
    args = [*full, *(a for result in results for a in result)]
    half, basis = full[0].shape
    side = jax.ShapeDtypeStruct((half, basis), F32)
    return pl.pallas_call(
        functools.partial(finish_kernel, scales),
        in_specs=[SMEM] + [WHOLE] * len(args),
        out_specs=[WHOLE] * 3,
        out_shape=[side, jax.ShapeDtypeStruct((8, half, basis), F32), side],
        cost_estimate=cost(20 * half * basis, 80 * half * basis),
        compiler_params=SMALL,
        name="finish",
    )(mask, *args)


def row_pairs(rows, shift):
    first = [(i, i + 1) for i in range(shift, rows - 1, 2)]
    return first + [(j, i) for i, j in first]


def beside(value, first):
    cols, sides = lax.axis_size("col"), lax.axis_size("aux")
    pairs = []
    for c in range(cols):
        other = c ^ 1 if first == 0 else ((c - 1) ^ 1) + 1
        for a in range(sides):
            inside = 0 <= other < cols
            pairs.append((c * sides + a, other * sides + a if inside else c * sides + (a + 1) % sides))
    return lax.ppermute(value, ("col", "aux"), pairs)


def local(coef_three, orbitals, density, pair_mask, *, full_q):
    _, _, q, width = coef_three.shape
    occupied, basis = orbitals.shape[2:]
    rows = lax.axis_size("row")
    coef = coef_three.reshape(q, width)
    quarter = occupied // 4
    small = max(1, 3 * quarter // 10)
    big = quarter - small
    parts = 2
    orb, dens = orbitals[0, 0], density[0, 0]
    ke0, ko0, se0, so0, kept0 = half_call(coef, orb, 0, parts, [quarter] * 4, 46)
    ke1, ko1, se1, se2, so1, so2, kept1 = half_call(
        coef, orb, 1, parts, [quarter, quarter, big, small, big, small], 46
    )
    full = full_call(kept1, dens, full_call(kept0, dens, ()))
    swap_sides = [(0, 1), (1, 0)]
    full = (full[0], lax.ppermute(full[1], "aux", swap_sides))
    near0 = (ke0, ko0, beside(ke0, 0), beside(ko0, 1))
    near1 = (ke1, ko1, beside(ke1, 0), beside(ko1, 1))
    plan = ((0, near0, se0, so0), (0, near1, se1, so1), (big * (q // parts), near1, se2, so2))
    results = []
    for shift in range(min(2, rows - 1)):
        swap = row_pairs(rows, shift)
        pieces = []
        for _, _, send_e, send_o in plan:
            y_e = lax.ppermute(send_e, "row", swap)
            y_o = lax.ppermute(send_o, "row", swap)
            pieces.append((y_e, y_o, beside(y_e, 0), beside(y_o, 1)))
        sums = ()
        for k, (start, near, _, _) in enumerate(plan):
            last = k == len(plan) - 1
            sums = meet_call(start, near, pieces[k], sums, last)
        mine, theirs = sums
        stay, even, odd = joined_call(mine, lax.ppermute(theirs, "aux", swap_sides))
        keep, send = across_call(stay, beside(even, 0), beside(odd, 1))
        results.append((keep, lax.ppermute(send, "row", swap)))
    scales = (
        1.0 / (full_q * occupied),
        1.0 / (full_q * occupied) ** 0.5,
        1.0 / (full_q * basis) ** 0.5,
    )
    exch_self, pair, exch_full = finish_call(pair_mask[0], full, results, scales)
    return exch_self[None, None], pair[None, None], exch_full[None, None]


def solution(mesh):
    in_specs = (
        P(("sys", "row"), "col", "aux", None),
        P(("sys", "row"), "col", None, None),
        P(("sys", "row"), "col", None, None),
        P(("sys", "row"), "col", None),
    )
    out_specs = (
        P(("sys", "row"), "col", "aux", None),
        P(("sys", "row"), "col", None, "aux", None),
        P(("sys", "row"), "col", "aux", None),
    )

    def whole(coef_three, orbitals, density, pair_mask):
        return jax.shard_map(
            functools.partial(local, full_q=coef_three.shape[2]),
            mesh=mesh,
            in_specs=in_specs,
            out_specs=out_specs,
            check_vma=False,
        )(coef_three, orbitals, density, pair_mask)

    return whole
```

```python
import functools

import jax
import jax.numpy as jnp
from jax import lax
from jax.experimental import pallas as pl
from jax.experimental.pallas import tpu as pltpu
from jax.sharding import PartitionSpec as P


LANES = 128
NT = (((1,), (1,)), ((), ()))
HBM = pl.BlockSpec(memory_space=pltpu.HBM)
WHOLE = pl.BlockSpec(memory_space=pltpu.VMEM)
SMEM = pl.BlockSpec(memory_space=pltpu.SMEM)
F32 = jnp.float32
BF16 = jnp.bfloat16
BATCH = 4
MIB = 2**20
SMALL = pltpu.CompilerParams(vmem_limit_bytes=12 * MIB)


def cost(flops, size):
    return pl.CostEstimate(flops=int(flops), bytes_accessed=int(size), transcendentals=0)


def odd_pitch(rows):
    return rows + 8 * (1 - (rows // 8) % 2)


def block(i, size):
    return pl.ds(pl.multiple_of(i * size, size), size)


def put_slabs(scratch, group, left, kept, i):
    height, (slabs, rows, lanes) = left.shape[0], scratch.shape
    pitch, q = rows // group, slabs * lanes
    for j in range(0, group, BATCH):
        first = pl.multiple_of((i * group + j) * q, BATCH * q)
        value = nt(left, kept[pl.ds(first, BATCH * q), :])
        for k in range(BATCH * slabs):
            at = (j + k // slabs) * pitch
            scratch[k % slabs, at : at + height, :] = value[:, k * lanes : (k + 1) * lanes]
    return pitch


def half_kernel(part, group, counts, coef, orb, *refs):
    outs, (kept, scratch, orb_ref, arrived) = refs[:-4], refs[-4:]
    occupied, basis = orb.shape
    slabs, _, lanes = scratch.shape
    q = slabs * lanes
    steps = basis // group
    quarter = occupied // 4
    flip_row = lax.axis_index("row") % 2
    flip_col = lax.axis_index("col") % 2
    copy = pltpu.make_async_copy(orb, orb_ref, arrived.at[steps])
    copy.start()

    @pl.loop(0, steps)
    def _(i):
        for j in range(group):
            k = i * group + j
            pltpu.make_async_copy(
                coef.at[part * q : (part + 1) * q, block(k, basis)], kept.at[block(k, q), :], arrived.at[i]
            ).start()

    copy.wait()
    orb = orb_ref[...]

    @pl.loop(0, steps)
    def _(i):
        here = kept.at[block(i, group * q), :]
        pltpu.make_async_copy(here, here, arrived.at[i]).wait()
        pitch = put_slabs(scratch, group, orb, kept, i)
        o = 0
        for out, count in zip(outs, counts):
            for k in range(count):
                send, turn = o // (2 * quarter), o // quarter % 2
                away = flip_row if send == 0 else 1 - flip_row
                over = 1 - flip_col if turn == 0 else flip_col
                row = o % quarter + 2 * quarter * away + quarter * over
                for h in range(slabs):
                    at = (k * slabs + h) * lanes
                    out[block(i, group), at : at + lanes] = scratch[h, pl.ds(row, group, stride=pitch), :].astype(BF16)
                o += 1


def half_call(coef, orb, part, parts, counts, group=32):
    q, width = coef.shape
    q //= parts
    occupied, basis = orb.shape
    shapes = [(basis, n * q) for n in counts] + [(basis * q, basis)]
    return pl.pallas_call(
        functools.partial(half_kernel, part, group, counts),
        in_specs=[HBM, HBM],
        out_specs=[WHOLE] * len(shapes),
        out_shape=[jax.ShapeDtypeStruct(shape, BF16) for shape in shapes],
        scratch_shapes=[
            pltpu.VMEM((q // LANES, group * odd_pitch(occupied), LANES), F32),
            pltpu.VMEM(orb.shape, BF16),
            pltpu.SemaphoreType.DMA((basis // group + 1,)),
        ],
        cost_estimate=cost(2 * q * width * occupied, 2 * q * width + 2 * occupied * basis * q),
        compiler_params=pltpu.CompilerParams(vmem_limit_bytes=16 * MIB),
    )(coef, orb)


def full_kernel(group, kept, dens_ref, *refs):
    before, outs, (turned, scratch) = refs[:-4], refs[-4:-2], refs[-2:]
    basis = dens_ref.shape[0]
    slabs, _, lanes = scratch.shape
    q = slabs * lanes
    dens = dens_ref[...].T

    @pl.loop(0, basis // group)
    def _(i):
        pitch = put_slabs(scratch, group, dens, kept, i)
        for s in range(basis):
            for h in range(slabs):
                at = s * q + h * lanes
                turned[block(i, group), at : at + lanes] = scratch[h, pl.ds(s, group, stride=pitch), :].astype(BF16)

    total = before[0][...] + before[1][...] if before else jnp.zeros((basis, basis), F32)
    span = basis // 2 * q
    for first in range(0, basis * q, span):
        total += jnp.dot(turned[:, first : first + span], kept[first : first + span, :], preferred_element_type=F32)
    half = basis // 2
    side = lax.axis_index("aux")
    if before:
        scratch[0, :basis, :] = total
        outs[0][...] = scratch[0, block(side, half), :]
        outs[1][...] = scratch[0, block(1 - side, half), :]
    else:
        outs[0][...] = total
        outs[1][...] = jnp.zeros_like(outs[1])


def full_call(kept, dens, before, group=64):
    basis = dens.shape[0]
    q = kept.shape[0] // basis
    height = basis // 2 if before else basis
    out = jax.ShapeDtypeStruct((height, basis), F32)
    args = [kept, dens, *before]
    return pl.pallas_call(
        functools.partial(full_kernel, group),
        in_specs=[WHOLE] * len(args),
        out_specs=[WHOLE] * 2,
        out_shape=[out, out],
        scratch_shapes=[
            pltpu.VMEM((basis, basis * q), BF16),
            pltpu.VMEM((q // LANES, group * odd_pitch(basis), LANES), F32),
        ],
        compiler_params=pltpu.CompilerParams(vmem_limit_bytes=16 * MIB),
        cost_estimate=cost(4 * q * basis**3, 2 * q * basis**2),
    )(*args)


def nt(left, right):
    return lax.dot_general(left, right, NT, preferred_element_type=F32)


def meet(start, x_e, x_o, far_e, far_o, y_e, y_o, farther_e, farther_o):
    here = slice(start, start + y_e.shape[1])
    near_e = jnp.concatenate([x_e[:, here], y_e[...]])
    near_o = jnp.concatenate([x_o[:, here], y_o[...]])
    even = nt(near_o, jnp.concatenate([far_e[:, here], farther_e[...]]))
    odd = nt(near_e, jnp.concatenate([far_o[:, here], farther_o[...]]))
    return even, odd, nt(near_e, near_e) + nt(near_o, near_o)


def meet_kernel(start, *refs):
    before, outs = refs[8:-3], refs[-3:]
    for k, value in enumerate(meet(start, *refs[:8])):
        outs[k][...] = value + before[k][...] if before else value


def last_kernel(start, *refs):
    before, (mine, theirs, lines) = refs[8:-3], refs[-3:]
    basis = mine.shape[2] // 2
    half = basis // 2
    sums = list(meet(start, *refs[:8]))
    for k, part in enumerate(before):
        sums[k] += part[...]
    for k in range(3):
        lines[k] = sums[k][:basis]
        lines[3 + k] = sums[k][basis:]
    for k in range(2):
        turned = sums[k].T
        lines[6 + 2 * k] = turned[:basis]
        lines[7 + 2 * k] = turned[basis:]
    side = lax.axis_index("aux")
    mine[...] = lines[:, pl.ds(pl.multiple_of(side * half, half), half), :]
    theirs[...] = lines[:, pl.ds(pl.multiple_of((1 - side) * half, half), half), :].astype(BF16)


def meet_call(start, xs, ys, before, last):
    basis, width = ys[0].shape
    two = jax.ShapeDtypeStruct((2 * basis, 2 * basis), F32)
    out = jax.ShapeDtypeStruct((10, basis // 2, 2 * basis), F32)
    args = [*xs, *ys, *before]
    shapes = [out, jax.ShapeDtypeStruct(out.shape, BF16)] if last else [two, two, two]
    return pl.pallas_call(
        functools.partial(last_kernel if last else meet_kernel, start),
        in_specs=[WHOLE] * len(args),
        out_specs=[WHOLE] * len(shapes),
        out_shape=shapes,
        scratch_shapes=[pltpu.VMEM((10, basis, 2 * basis), F32)] if last else [],
        cost_estimate=cost(24 * basis * basis * width, 16 * basis * width),
        compiler_params=SMALL,
    )(*args)


def joined_kernel(mine, theirs, stay, even, odd):
    stay[...] = mine[0:6] + theirs[0:6].astype(F32)
    even[...] = (mine[6:8] + theirs[6:8].astype(F32)).astype(BF16)
    odd[...] = (mine[8:10] + theirs[8:10].astype(F32)).astype(BF16)


def joined_call(mine, theirs):
    _, half, two = mine.shape
    onward = jax.ShapeDtypeStruct((2, half, two), BF16)
    return pl.pallas_call(
        joined_kernel,
        in_specs=[WHOLE] * 2,
        out_specs=[WHOLE] * 3,
        out_shape=[jax.ShapeDtypeStruct((6, half, two), F32), onward, onward],
        cost_estimate=cost(mine.size, 12 * mine.size),
        compiler_params=SMALL,
        name="joined",
    )(mine, theirs)


def across_kernel(stay, even, odd, keep, send):
    keep[0] = stay[0] + even[0].astype(F32)
    keep[1] = stay[1] + odd[0].astype(F32)
    keep[2] = stay[2]
    send[0] = (stay[3] + even[1].astype(F32)).astype(BF16)
    send[1] = (stay[4] + odd[1].astype(F32)).astype(BF16)
    send[2] = stay[5].astype(BF16)


def across_call(stay, even, odd):
    _, half, two = stay.shape
    return pl.pallas_call(
        across_kernel,
        in_specs=[WHOLE] * 3,
        out_specs=[WHOLE] * 2,
        out_shape=[jax.ShapeDtypeStruct((3, half, two), F32), jax.ShapeDtypeStruct((3, half, two), BF16)],
        cost_estimate=cost(stay.size, 8 * stay.size),
        compiler_params=SMALL,
        name="across",
    )(stay, even, odd)


def factor_kernel(pair_scale, mask, out):
    row, col = lax.axis_index("row"), lax.axis_index("col")
    rows, cols = lax.axis_size("row"), lax.axis_size("col")
    for d in range(8):
        k = d + d // 4
        r, c = row + k // 3 - 1, col + k % 3 - 1
        inside = (r >= 0) & (r < rows) & (c >= 0) & (c < cols)
        factor = jnp.where(inside, mask[0, d].astype(F32) * pair_scale, 0.0)
        out[d] = jnp.full(out.shape[1:], factor, F32)


def factor_call(mask, basis, pair_scale):
    return pl.pallas_call(
        functools.partial(factor_kernel, pair_scale),
        in_specs=[SMEM],
        out_specs=WHOLE,
        out_shape=jax.ShapeDtypeStruct((8, 8, basis), F32),
        cost_estimate=cost(64, 64 * basis),
        compiler_params=SMALL,
        name="factor",
    )(mask)


def finish_kernel(scales, factors, full_mine, full_theirs, *refs):
    self_scale, full_scale = scales
    ins, (self_out, pair_out, full_out) = refs[:-3], refs[-3:]
    basis = self_out.shape[1]
    row, col = lax.axis_index("row"), lax.axis_index("col")
    even_right = 1 - col % 2

    def put(down, right, value):
        d = (down + 1) * 3 + right + 1
        d = d - (d > 4).astype(jnp.int32)
        pair_out[d] = value * factors[d, 0:1, :]

    to_even, to_odd = 2 * even_right - 1, 1 - 2 * even_right
    full_out[...] = (full_mine[...] + full_theirs[...]) * full_scale
    if len(ins) == 2:
        for d in range(3):
            pair_out[jnp.where(row % 2 == 0, d, 5 + d)] = jnp.zeros_like(full_mine)
    for shift in range(len(ins) // 2):
        keep, got = ins[2 * shift : 2 * shift + 2]
        down = 2 * (row % 2 == shift).astype(jnp.int32) - 1
        own = [keep[k, :, :basis] + got[k, :, basis:].astype(F32) for k in range(3)]
        other = [keep[k, :, basis:] + got[k, :, :basis].astype(F32) for k in range(3)]
        put(down, to_even, other[0])
        put(down, to_odd, other[1])
        put(down, 0, other[2])
        if shift == 0:
            put(0, to_even, own[0])
            put(0, to_odd, own[1])
            self_out[...] = own[2] * self_scale


def finish_call(factors, full, results, scales):
    args = [factors, *full, *(a for result in results for a in result)]
    half, basis = full[0].shape
    side = jax.ShapeDtypeStruct((half, basis), F32)
    return pl.pallas_call(
        functools.partial(finish_kernel, scales),
        in_specs=[WHOLE] * len(args),
        out_specs=[WHOLE] * 3,
        out_shape=[side, jax.ShapeDtypeStruct((8, half, basis), F32), side],
        cost_estimate=cost(20 * half * basis, 80 * half * basis),
        compiler_params=SMALL,
        name="finish",
    )(*args)


def in_hbm(value):
    return pltpu.with_memory_space_constraint(value, pltpu.HBM)


def row_pairs(rows, shift):
    first = [(i, i + 1) for i in range(shift, rows - 1, 2)]
    return first + [(j, i) for i, j in first]


def beside(value, first):
    cols, sides = lax.axis_size("col"), lax.axis_size("aux")
    pairs = []
    for c in range(cols):
        other = c ^ 1 if first == 0 else ((c - 1) ^ 1) + 1
        for a in range(sides):
            inside = 0 <= other < cols
            pairs.append((c * sides + a, other * sides + a if inside else c * sides + (a + 1) % sides))
    return lax.ppermute(value, ("col", "aux"), pairs)


def local(coef_three, orbitals, density, pair_mask, *, full_q):
    _, _, q, width = coef_three.shape
    occupied, basis = orbitals.shape[2:]
    rows = lax.axis_size("row")
    coef = in_hbm(coef_three.reshape(q, width))
    quarter = occupied // 4
    small = max(1, 3 * quarter // 10)
    big = quarter - small
    parts = 2
    orb, dens = in_hbm(orbitals[0, 0]), density[0, 0]
    ke0, ko0, se0, so0, kept0 = half_call(coef, orb, 0, parts, [quarter] * 4)
    ke1, ko1, se1, se2, so1, so2, kept1 = half_call(
        coef, orb, 1, parts, [quarter, quarter, big, small, big, small]
    )
    full = full_call(kept1, dens, full_call(kept0, dens, ()))
    swap_sides = [(0, 1), (1, 0)]
    full = (full[0], lax.ppermute(full[1], "aux", swap_sides))
    near0 = (ke0, ko0, beside(ke0, 0), beside(ko0, 1))
    near1 = (ke1, ko1, beside(ke1, 0), beside(ko1, 1))
    plan = ((0, near0, se0, so0), (0, near1, se1, so1), (big * (q // parts), near1, se2, so2))
    results = []
    for shift in range(min(2, rows - 1)):
        swap = row_pairs(rows, shift)
        pieces = []
        for _, _, send_e, send_o in plan:
            y_e = lax.ppermute(send_e, "row", swap)
            y_o = lax.ppermute(send_o, "row", swap)
            pieces.append((y_e, y_o, beside(y_e, 0), beside(y_o, 1)))
        sums = ()
        for k, (start, near, _, _) in enumerate(plan):
            last = k == len(plan) - 1
            sums = meet_call(start, near, pieces[k], sums, last)
        mine, theirs = sums
        stay, even, odd = joined_call(mine, lax.ppermute(theirs, "aux", swap_sides))
        keep, send = across_call(stay, beside(even, 0), beside(odd, 1))
        results.append((keep, lax.ppermute(send, "row", swap)))
    factors = factor_call(pair_mask[0], basis, 1.0 / (full_q * occupied) ** 0.5)
    scales = (1.0 / (full_q * occupied), 1.0 / (full_q * basis) ** 0.5)
    exch_self, pair, exch_full = finish_call(factors, full, results, scales)
    return exch_self[None, None], pair[None, None], exch_full[None, None]


def solution(mesh):
    in_specs = (
        P(("sys", "row"), "col", "aux", None),
        P(("sys", "row"), "col", None, None),
        P(("sys", "row"), "col", None, None),
        P(("sys", "row"), "col", None),
    )
    out_specs = (
        P(("sys", "row"), "col", "aux", None),
        P(("sys", "row"), "col", None, "aux", None),
        P(("sys", "row"), "col", "aux", None),
    )

    def whole(coef_three, orbitals, density, pair_mask):
        return jax.shard_map(
            functools.partial(local, full_q=coef_three.shape[2]),
            mesh=mesh,
            in_specs=in_specs,
            out_specs=out_specs,
            check_vma=False,
        )(coef_three, orbitals, density, pair_mask)

    return whole
```

```python
import functools

import jax
import jax.numpy as jnp
from jax import lax
from jax.experimental import pallas as pl
from jax.experimental.pallas import tpu as pltpu
from jax.sharding import PartitionSpec as P


LANES = 128
NT = (((1,), (1,)), ((), ()))
HBM = pl.BlockSpec(memory_space=pltpu.HBM)
WHOLE = pl.BlockSpec(memory_space=pltpu.VMEM)
SMEM = pl.BlockSpec(memory_space=pltpu.SMEM)
F32 = jnp.float32
BF16 = jnp.bfloat16
BATCH = 4
MIB = 2**20
SMALL = pltpu.CompilerParams(vmem_limit_bytes=12 * MIB)


def cost(flops, size):
    return pl.CostEstimate(flops=int(flops), bytes_accessed=int(size), transcendentals=0)


def odd_pitch(rows):
    return rows + 8 * (1 - (rows // 8) % 2)


def block(i, size):
    return pl.ds(pl.multiple_of(i * size, size), size)


def put_slabs(scratch, group, left, kept, i):
    height, (slabs, rows, lanes) = left.shape[0], scratch.shape
    pitch, q = rows // group, slabs * lanes
    for j in range(0, group, BATCH):
        first = pl.multiple_of((i * group + j) * q, BATCH * q)
        value = nt(left, kept[pl.ds(first, BATCH * q), :])
        for k in range(BATCH * slabs):
            at = (j + k // slabs) * pitch
            scratch[k % slabs, at : at + height, :] = value[:, k * lanes : (k + 1) * lanes]
    return pitch


def half_kernel(part, group, counts, coef, orb, *refs):
    outs, (kept, scratch, orb_ref, arrived) = refs[:-4], refs[-4:]
    occupied, basis = orb.shape
    slabs, _, lanes = scratch.shape
    q = slabs * lanes
    steps = basis // group
    quarter = occupied // 4
    flip_row = lax.axis_index("row") % 2
    flip_col = lax.axis_index("col") % 2
    copy = pltpu.make_async_copy(orb, orb_ref, arrived.at[steps])
    copy.start()

    @pl.loop(0, steps)
    def _(i):
        for j in range(group):
            k = i * group + j
            pltpu.make_async_copy(
                coef.at[part * q : (part + 1) * q, block(k, basis)], kept.at[block(k, q), :], arrived.at[i]
            ).start()

    copy.wait()
    orb = orb_ref[...]

    @pl.loop(0, steps)
    def _(i):
        here = kept.at[block(i, group * q), :]
        pltpu.make_async_copy(here, here, arrived.at[i]).wait()
        pitch = put_slabs(scratch, group, orb, kept, i)
        o = 0
        for out, count in zip(outs, counts):
            for k in range(count):
                send, turn = o // (2 * quarter), o // quarter % 2
                away = flip_row if send == 0 else 1 - flip_row
                over = 1 - flip_col if turn == 0 else flip_col
                row = o % quarter + 2 * quarter * away + quarter * over
                for h in range(slabs):
                    at = (k * slabs + h) * lanes
                    out[block(i, group), at : at + lanes] = scratch[h, pl.ds(row, group, stride=pitch), :].astype(BF16)
                o += 1


def half_call(coef, orb, part, parts, counts, group=32):
    q, width = coef.shape
    q //= parts
    occupied, basis = orb.shape
    shapes = [(basis, n * q) for n in counts] + [(basis * q, basis)]
    return pl.pallas_call(
        functools.partial(half_kernel, part, group, counts),
        in_specs=[HBM, HBM],
        out_specs=[WHOLE] * len(shapes),
        out_shape=[jax.ShapeDtypeStruct(shape, BF16) for shape in shapes],
        scratch_shapes=[
            pltpu.VMEM((q // LANES, group * odd_pitch(occupied), LANES), F32),
            pltpu.VMEM(orb.shape, BF16),
            pltpu.SemaphoreType.DMA((basis // group + 1,)),
        ],
        cost_estimate=cost(2 * q * width * occupied, 2 * q * width + 2 * occupied * basis * q),
        compiler_params=pltpu.CompilerParams(vmem_limit_bytes=16 * MIB),
    )(coef, orb)


def full_kernel(group, kept, dens_ref, *refs):
    before, outs, (turned, scratch) = refs[:-4], refs[-4:-2], refs[-2:]
    basis = dens_ref.shape[0]
    slabs, _, lanes = scratch.shape
    q = slabs * lanes
    dens = dens_ref[...].T

    @pl.loop(0, basis // group)
    def _(i):
        pitch = put_slabs(scratch, group, dens, kept, i)
        for s in range(basis):
            for h in range(slabs):
                at = s * q + h * lanes
                turned[block(i, group), at : at + lanes] = scratch[h, pl.ds(s, group, stride=pitch), :].astype(BF16)

    total = before[0][...] + before[1][...] if before else jnp.zeros((basis, basis), F32)
    span = basis // 2 * q
    for first in range(0, basis * q, span):
        total += jnp.dot(turned[:, first : first + span], kept[first : first + span, :], preferred_element_type=F32)
    half = basis // 2
    side = lax.axis_index("aux")
    if before:
        scratch[0, :basis, :] = total
        outs[0][...] = scratch[0, block(side, half), :]
        outs[1][...] = scratch[0, block(1 - side, half), :]
    else:
        outs[0][...] = total
        outs[1][...] = jnp.zeros_like(outs[1])


def full_call(kept, dens, before, group=64):
    basis = dens.shape[0]
    q = kept.shape[0] // basis
    height = basis // 2 if before else basis
    out = jax.ShapeDtypeStruct((height, basis), F32)
    args = [kept, dens, *before]
    return pl.pallas_call(
        functools.partial(full_kernel, group),
        in_specs=[WHOLE] * len(args),
        out_specs=[WHOLE] * 2,
        out_shape=[out, out],
        scratch_shapes=[
            pltpu.VMEM((basis, basis * q), BF16),
            pltpu.VMEM((q // LANES, group * odd_pitch(basis), LANES), F32),
        ],
        compiler_params=pltpu.CompilerParams(vmem_limit_bytes=16 * MIB),
        cost_estimate=cost(4 * q * basis**3, 2 * q * basis**2),
    )(*args)


def nt(left, right):
    return lax.dot_general(left, right, NT, preferred_element_type=F32)


def over(upper, lower):
    return jnp.concatenate([upper, lower])


def beside_each(refs):
    return jnp.concatenate([r[...] for r in refs], axis=1)


def first_kernel(x_e, x_o, far_e, far_o, y_e, y_o, farther_e, farther_o, even, odd, square):
    near_e, near_o = over(x_e[...], y_e[...]), over(x_o[...], y_o[...])
    even[...] = nt(near_o, over(far_e[...], farther_e[...]))
    odd[...] = nt(near_e, over(far_o[...], farther_o[...]))
    square[...] = nt(near_e, near_e) + nt(near_o, near_o)


def middle_kernel(count, *refs):
    (x_e, x_o, far_e, y_o), refs = refs[:4], refs[4:]
    y_e, farther_e, (even, square, even_out, square_out) = refs[:count], refs[count:-4], refs[-4:]
    width = sum(r.shape[1] for r in y_e)
    near_e, near_o = over(x_e[:, :width], beside_each(y_e)), over(x_o[...], y_o[...])
    even_out[...] = even[...] + nt(near_o[:, :width], over(far_e[:, :width], beside_each(farther_e)))
    square_out[...] = square[...] + nt(near_e, near_e) + nt(near_o, near_o)


def last_kernel(count, *refs):
    (x_e, x_o, far_e, far_o, y_o, farther_o), refs = refs[:6], refs[6:]
    y_e, (farther_e, even, odd, square, mine, theirs, lines) = refs[:count], refs[count:]
    basis = mine.shape[2] // 2
    half = basis // 2
    tail = slice(x_e.shape[1] - farther_e.shape[1], x_e.shape[1])
    near_e = over(x_e[...], beside_each(y_e))
    sums = [
        even[...] + nt(over(x_o[:, tail], y_o[:, tail]), over(far_e[:, tail], farther_e[...])),
        odd[...] + nt(near_e, over(far_o[...], farther_o[...])),
        square[...] + nt(near_e[:, tail], near_e[:, tail]),
    ]
    for k in range(3):
        lines[k] = sums[k][:basis]
        lines[3 + k] = sums[k][basis:]
    for k in range(2):
        turned = sums[k].T
        lines[6 + 2 * k] = turned[:basis]
        lines[7 + 2 * k] = turned[basis:]
    side = lax.axis_index("aux")
    mine[...] = lines[:, block(side, half), :]
    theirs[...] = lines[:, block(1 - side, half), :].astype(BF16)


def sum_call(kernel, args, shapes, width, scratch=()):
    basis = args[0].shape[0]
    return pl.pallas_call(
        kernel,
        in_specs=[WHOLE] * len(args),
        out_specs=[WHOLE] * len(shapes),
        out_shape=shapes,
        scratch_shapes=scratch,
        cost_estimate=cost(24 * basis * basis * width, 16 * basis * width),
        compiler_params=SMALL,
    )(*args)


def joined_kernel(mine, theirs, stay, even, odd):
    stay[...] = mine[0:6] + theirs[0:6].astype(F32)
    even[...] = (mine[6:8] + theirs[6:8].astype(F32)).astype(BF16)
    odd[...] = (mine[8:10] + theirs[8:10].astype(F32)).astype(BF16)


def joined_call(mine, theirs):
    _, half, two = mine.shape
    onward = jax.ShapeDtypeStruct((2, half, two), BF16)
    return pl.pallas_call(
        joined_kernel,
        in_specs=[WHOLE] * 2,
        out_specs=[WHOLE] * 3,
        out_shape=[jax.ShapeDtypeStruct((6, half, two), F32), onward, onward],
        cost_estimate=cost(mine.size, 12 * mine.size),
        compiler_params=SMALL,
        name="joined",
    )(mine, theirs)


def across_kernel(stay, even, odd, keep, send):
    keep[0] = stay[0] + even[0].astype(F32)
    keep[1] = stay[1] + odd[0].astype(F32)
    keep[2] = stay[2]
    send[0] = (stay[3] + even[1].astype(F32)).astype(BF16)
    send[1] = (stay[4] + odd[1].astype(F32)).astype(BF16)
    send[2] = stay[5].astype(BF16)


def across_call(stay, even, odd):
    _, half, two = stay.shape
    return pl.pallas_call(
        across_kernel,
        in_specs=[WHOLE] * 3,
        out_specs=[WHOLE] * 2,
        out_shape=[jax.ShapeDtypeStruct((3, half, two), F32), jax.ShapeDtypeStruct((3, half, two), BF16)],
        cost_estimate=cost(stay.size, 8 * stay.size),
        compiler_params=SMALL,
        name="across",
    )(stay, even, odd)


def factor_kernel(pair_scale, mask, out):
    row, col = lax.axis_index("row"), lax.axis_index("col")
    rows, cols = lax.axis_size("row"), lax.axis_size("col")
    for d in range(8):
        k = d + d // 4
        r, c = row + k // 3 - 1, col + k % 3 - 1
        inside = (r >= 0) & (r < rows) & (c >= 0) & (c < cols)
        factor = jnp.where(inside, mask[0, d].astype(F32) * pair_scale, 0.0)
        out[d] = jnp.full(out.shape[1:], factor, F32)


def factor_call(mask, basis, pair_scale):
    return pl.pallas_call(
        functools.partial(factor_kernel, pair_scale),
        in_specs=[SMEM],
        out_specs=WHOLE,
        out_shape=jax.ShapeDtypeStruct((8, 8, basis), F32),
        cost_estimate=cost(64, 64 * basis),
        compiler_params=SMALL,
        name="factor",
    )(mask)


def finish_kernel(scales, factors, full_mine, full_theirs, *refs):
    self_scale, full_scale = scales
    ins, (self_out, pair_out, full_out) = refs[:-3], refs[-3:]
    basis = self_out.shape[1]
    row, col = lax.axis_index("row"), lax.axis_index("col")
    even_right = 1 - col % 2

    def put(down, right, value):
        d = (down + 1) * 3 + right + 1
        d = d - (d > 4).astype(jnp.int32)
        pair_out[d] = value * factors[d, 0:1, :]

    to_even, to_odd = 2 * even_right - 1, 1 - 2 * even_right
    full_out[...] = (full_mine[...] + full_theirs[...]) * full_scale
    if len(ins) == 2:
        for d in range(3):
            pair_out[jnp.where(row % 2 == 0, d, 5 + d)] = jnp.zeros_like(full_mine)
    for shift in range(len(ins) // 2):
        keep, got = ins[2 * shift : 2 * shift + 2]
        down = 2 * (row % 2 == shift).astype(jnp.int32) - 1
        own = [keep[k, :, :basis] + got[k, :, basis:].astype(F32) for k in range(3)]
        other = [keep[k, :, basis:] + got[k, :, :basis].astype(F32) for k in range(3)]
        put(down, to_even, other[0])
        put(down, to_odd, other[1])
        put(down, 0, other[2])
        if shift == 0:
            put(0, to_even, own[0])
            put(0, to_odd, own[1])
            self_out[...] = own[2] * self_scale


def finish_call(factors, full, results, scales):
    args = [factors, *full, *(a for result in results for a in result)]
    half, basis = full[0].shape
    side = jax.ShapeDtypeStruct((half, basis), F32)
    return pl.pallas_call(
        functools.partial(finish_kernel, scales),
        in_specs=[WHOLE] * len(args),
        out_specs=[WHOLE] * 3,
        out_shape=[side, jax.ShapeDtypeStruct((8, half, basis), F32), side],
        cost_estimate=cost(20 * half * basis, 80 * half * basis),
        compiler_params=SMALL,
        name="finish",
    )(*args)


def in_hbm(value):
    return pltpu.with_memory_space_constraint(value, pltpu.HBM)


def row_pairs(rows, shift):
    first = [(i, i + 1) for i in range(shift, rows - 1, 2)]
    return first + [(j, i) for i, j in first]


def beside(value, first):
    cols, sides = lax.axis_size("col"), lax.axis_size("aux")
    pairs = []
    for c in range(cols):
        other = c ^ 1 if first == 0 else ((c - 1) ^ 1) + 1
        for a in range(sides):
            inside = 0 <= other < cols
            pairs.append((c * sides + a, other * sides + a if inside else c * sides + (a + 1) % sides))
    return lax.ppermute(value, ("col", "aux"), pairs)


def local(coef_three, orbitals, density, pair_mask, *, full_q):
    _, _, q, width = coef_three.shape
    occupied, basis = orbitals.shape[2:]
    rows = lax.axis_size("row")
    coef = in_hbm(coef_three.reshape(q, width))
    quarter = occupied // 4
    small = max(1, 3 * quarter // 10)
    sizes = [quarter - 2 * small, small, small]
    count = len(sizes)
    parts = 2
    orb, dens = in_hbm(orbitals[0, 0]), density[0, 0]
    ke0, ko0, se0, so0, kept0 = half_call(coef, orb, 0, parts, [quarter] * 4)
    ke1, ko1, *se1, so1, kept1 = half_call(coef, orb, 1, parts, [quarter, quarter, *sizes, quarter])
    full = full_call(kept1, dens, full_call(kept0, dens, ()))
    swap_sides = [(0, 1), (1, 0)]
    full = (full[0], lax.ppermute(full[1], "aux", swap_sides))
    fe0, fo0 = beside(ke0, 0), beside(ko0, 1)
    fe1, fo1 = beside(ke1, 0), beside(ko1, 1)
    two = jax.ShapeDtypeStruct((2 * basis, 2 * basis), F32)
    shape = (10, basis // 2, 2 * basis)
    ends = [jax.ShapeDtypeStruct(shape, F32), jax.ShapeDtypeStruct(shape, BF16)]
    lines = [pltpu.VMEM((10, basis, 2 * basis), F32)]
    part_q = q // parts
    results = []
    for shift in range(min(2, rows - 1)):
        swap = row_pairs(rows, shift)
        ye0, yo0 = lax.ppermute(se0, "row", swap), lax.ppermute(so0, "row", swap)
        yo1 = lax.ppermute(so1, "row", swap)
        ye1 = [lax.ppermute(send, "row", swap) for send in se1]
        ge0, go0 = beside(ye0, 0), beside(yo0, 1)
        go1 = beside(yo1, 1)
        ge1 = [beside(y, 0) for y in ye1]
        args = [ke0, ko0, fe0, fo0, ye0, yo0, ge0, go0]
        even, odd, square = sum_call(first_kernel, args, [two] * 3, quarter * part_q)
        args = [ke1, ko1, fe1, yo1, *ye1[:-1], *ge1[:-1], even, square]
        kernel = functools.partial(middle_kernel, count - 1)
        even, square = sum_call(kernel, args, [two] * 2, quarter * part_q)
        args = [ke1, ko1, fe1, fo1, yo1, go1, *ye1, ge1[-1], even, odd, square]
        kernel = functools.partial(last_kernel, count)
        mine, theirs = sum_call(kernel, args, ends, quarter * part_q, lines)
        stay, even, odd = joined_call(mine, lax.ppermute(theirs, "aux", swap_sides))
        keep, send = across_call(stay, beside(even, 0), beside(odd, 1))
        results.append((keep, lax.ppermute(send, "row", swap)))
    factors = factor_call(pair_mask[0], basis, 1.0 / (full_q * occupied) ** 0.5)
    scales = (1.0 / (full_q * occupied), 1.0 / (full_q * basis) ** 0.5)
    exch_self, pair, exch_full = finish_call(factors, full, results, scales)
    return exch_self[None, None], pair[None, None], exch_full[None, None]


def solution(mesh):
    in_specs = (
        P(("sys", "row"), "col", "aux", None),
        P(("sys", "row"), "col", None, None),
        P(("sys", "row"), "col", None, None),
        P(("sys", "row"), "col", None),
    )
    out_specs = (
        P(("sys", "row"), "col", "aux", None),
        P(("sys", "row"), "col", None, "aux", None),
        P(("sys", "row"), "col", "aux", None),
    )

    def whole(coef_three, orbitals, density, pair_mask):
        return jax.shard_map(
            functools.partial(local, full_q=coef_three.shape[2]),
            mesh=mesh,
            in_specs=in_specs,
            out_specs=out_specs,
            check_vma=False,
        )(coef_three, orbitals, density, pair_mask)

    return whole
```

```python
import functools

import jax
import jax.numpy as jnp
from jax import lax
from jax.experimental import pallas as pl
from jax.experimental.pallas import tpu as pltpu
from jax.sharding import PartitionSpec as P


LANES = 128
NT = (((1,), (1,)), ((), ()))
HBM = pl.BlockSpec(memory_space=pltpu.HBM)
WHOLE = pl.BlockSpec(memory_space=pltpu.VMEM)
SMEM = pl.BlockSpec(memory_space=pltpu.SMEM)
F32 = jnp.float32
BF16 = jnp.bfloat16
BATCH = 4
MIB = 2**20
SMALL = pltpu.CompilerParams(vmem_limit_bytes=12 * MIB)


def cost(flops, size):
    return pl.CostEstimate(flops=int(flops), bytes_accessed=int(size), transcendentals=0)


def odd_pitch(rows):
    return rows + 8 * (1 - (rows // 8) % 2)


def block(i, size):
    return pl.ds(pl.multiple_of(i * size, size), size)


def put_slabs(scratch, group, left, kept, i):
    height, (slabs, rows, lanes) = left.shape[0], scratch.shape
    pitch, q = rows // group, slabs * lanes
    for j in range(0, group, BATCH):
        first = pl.multiple_of((i * group + j) * q, BATCH * q)
        value = nt(left, kept[pl.ds(first, BATCH * q), :])
        for k in range(BATCH * slabs):
            at = (j + k // slabs) * pitch
            scratch[k % slabs, at : at + height, :] = value[:, k * lanes : (k + 1) * lanes]
    return pitch


def half_kernel(part, group, counts, coef, orb, *refs):
    outs, (kept, scratch, orb_ref, arrived) = refs[:-4], refs[-4:]
    occupied, basis = orb.shape
    slabs, _, lanes = scratch.shape
    q = slabs * lanes
    steps = basis // group
    quarter = occupied // 4
    flip_row = lax.axis_index("row") % 2
    flip_col = lax.axis_index("col") % 2
    copy = pltpu.make_async_copy(orb, orb_ref, arrived.at[steps])
    copy.start()

    @pl.loop(0, steps)
    def _(i):
        for j in range(group):
            k = i * group + j
            pltpu.make_async_copy(
                coef.at[part * q : (part + 1) * q, block(k, basis)], kept.at[block(k, q), :], arrived.at[i]
            ).start()

    copy.wait()
    orb = orb_ref[...]

    @pl.loop(0, steps)
    def _(i):
        here = kept.at[block(i, group * q), :]
        pltpu.make_async_copy(here, here, arrived.at[i]).wait()
        pitch = put_slabs(scratch, group, orb, kept, i)
        o = 0
        for out, count in zip(outs, counts):
            for k in range(count):
                send, turn = o // (2 * quarter), o // quarter % 2
                away = flip_row if send == 0 else 1 - flip_row
                over = 1 - flip_col if turn == 0 else flip_col
                row = o % quarter + 2 * quarter * away + quarter * over
                for h in range(slabs):
                    at = (k * slabs + h) * lanes
                    out[block(i, group), at : at + lanes] = scratch[h, pl.ds(row, group, stride=pitch), :].astype(BF16)
                o += 1


def half_call(coef, orb, part, parts, counts, group=32):
    q, width = coef.shape
    q //= parts
    occupied, basis = orb.shape
    shapes = [(basis, n * q) for n in counts] + [(basis * q, basis)]
    return pl.pallas_call(
        functools.partial(half_kernel, part, group, counts),
        in_specs=[HBM, HBM],
        out_specs=[WHOLE] * len(shapes),
        out_shape=[jax.ShapeDtypeStruct(shape, BF16) for shape in shapes],
        scratch_shapes=[
            pltpu.VMEM((q // LANES, group * odd_pitch(occupied), LANES), F32),
            pltpu.VMEM(orb.shape, BF16),
            pltpu.SemaphoreType.DMA((basis // group + 1,)),
        ],
        cost_estimate=cost(2 * q * width * occupied, 2 * q * width + 2 * occupied * basis * q),
        compiler_params=pltpu.CompilerParams(vmem_limit_bytes=16 * MIB),
    )(coef, orb)


def full_kernel(group, kept, dens_ref, *refs):
    before, outs, (turned, scratch) = refs[:-4], refs[-4:-2], refs[-2:]
    basis = dens_ref.shape[0]
    slabs, _, lanes = scratch.shape
    q = slabs * lanes
    dens = dens_ref[...].T

    @pl.loop(0, basis // group)
    def _(i):
        pitch = put_slabs(scratch, group, dens, kept, i)
        for s in range(basis):
            for h in range(slabs):
                at = s * q + h * lanes
                turned[block(i, group), at : at + lanes] = scratch[h, pl.ds(s, group, stride=pitch), :].astype(BF16)

    total = before[0][...] + before[1][...] if before else jnp.zeros((basis, basis), F32)
    span = basis // 2 * q
    for first in range(0, basis * q, span):
        total += jnp.dot(turned[:, first : first + span], kept[first : first + span, :], preferred_element_type=F32)
    half = basis // 2
    side = lax.axis_index("aux")
    if before:
        scratch[0, :basis, :] = total
        outs[0][...] = scratch[0, block(side, half), :]
        outs[1][...] = scratch[0, block(1 - side, half), :]
    else:
        outs[0][...] = total
        outs[1][...] = jnp.zeros_like(outs[1])


def full_call(kept, dens, before, group=64):
    basis = dens.shape[0]
    q = kept.shape[0] // basis
    height = basis // 2 if before else basis
    out = jax.ShapeDtypeStruct((height, basis), F32)
    args = [kept, dens, *before]
    return pl.pallas_call(
        functools.partial(full_kernel, group),
        in_specs=[WHOLE] * len(args),
        out_specs=[WHOLE] * 2,
        out_shape=[out, out],
        scratch_shapes=[
            pltpu.VMEM((basis, basis * q), BF16),
            pltpu.VMEM((q // LANES, group * odd_pitch(basis), LANES), F32),
        ],
        compiler_params=pltpu.CompilerParams(vmem_limit_bytes=16 * MIB),
        cost_estimate=cost(4 * q * basis**3, 2 * q * basis**2),
    )(*args)


def nt(left, right):
    return lax.dot_general(left, right, NT, preferred_element_type=F32)


def meet(start, x_e, x_o, far_e, far_o, y_e, y_o, farther_e, farther_o):
    here = slice(start, start + y_e.shape[1])
    near_e = jnp.concatenate([x_e[:, here], y_e[...]])
    near_o = jnp.concatenate([x_o[:, here], y_o[...]])
    even = nt(near_o, jnp.concatenate([far_e[:, here], farther_e[...]]))
    odd = nt(near_e, jnp.concatenate([far_o[:, here], farther_o[...]]))
    return even, odd, nt(near_e, near_e) + nt(near_o, near_o)


def meet_kernel(start, *refs):
    before, outs = refs[8:-3], refs[-3:]
    for k, value in enumerate(meet(start, *refs[:8])):
        outs[k][...] = value + before[k][...] if before else value


def last_kernel(start, *refs):
    before, (mine, theirs, lines) = refs[8:-3], refs[-3:]
    basis = mine.shape[2] // 2
    half = basis // 2
    sums = list(meet(start, *refs[:8]))
    for k, part in enumerate(before):
        sums[k] += part[...]
    for k in range(3):
        lines[k] = sums[k][:basis]
        lines[3 + k] = sums[k][basis:]
    for k in range(2):
        turned = sums[k].T
        lines[6 + 2 * k] = turned[:basis]
        lines[7 + 2 * k] = turned[basis:]
    side = lax.axis_index("aux")
    mine[...] = lines[:, pl.ds(pl.multiple_of(side * half, half), half), :]
    theirs[...] = lines[:, pl.ds(pl.multiple_of((1 - side) * half, half), half), :].astype(BF16)


def meet_call(start, xs, ys, before, last):
    basis, width = ys[0].shape
    two = jax.ShapeDtypeStruct((2 * basis, 2 * basis), F32)
    out = jax.ShapeDtypeStruct((10, basis // 2, 2 * basis), F32)
    args = [*xs, *ys, *before]
    shapes = [out, jax.ShapeDtypeStruct(out.shape, BF16)] if last else [two, two, two]
    return pl.pallas_call(
        functools.partial(last_kernel if last else meet_kernel, start),
        in_specs=[WHOLE] * len(args),
        out_specs=[WHOLE] * len(shapes),
        out_shape=shapes,
        scratch_shapes=[pltpu.VMEM((10, basis, 2 * basis), F32)] if last else [],
        cost_estimate=cost(24 * basis * basis * width, 16 * basis * width),
        compiler_params=SMALL,
    )(*args)


def joined_kernel(mine, theirs, stay, even, odd, send):
    stay[...] = mine[0:3] + theirs[0:3].astype(F32)
    send[...] = (mine[3:6] + theirs[3:6].astype(F32)).astype(BF16)
    even[...] = (mine[6:8] + theirs[6:8].astype(F32)).astype(BF16)
    odd[...] = (mine[8:10] + theirs[8:10].astype(F32)).astype(BF16)


def joined_call(mine, theirs):
    _, half, two = mine.shape
    onward = jax.ShapeDtypeStruct((2, half, two), BF16)
    stay = jax.ShapeDtypeStruct((3, half, two), F32)
    return pl.pallas_call(
        joined_kernel,
        in_specs=[WHOLE] * 2,
        out_specs=[WHOLE] * 4,
        out_shape=[stay, onward, onward, jax.ShapeDtypeStruct((3, half, two), BF16)],
        cost_estimate=cost(mine.size, 12 * mine.size),
        compiler_params=SMALL,
        name="joined",
    )(mine, theirs)


def across_kernel(even, odd, send):
    send[0] = even[1]
    send[1] = odd[1]


def across_call(even, odd):
    return pl.pallas_call(
        across_kernel,
        in_specs=[WHOLE] * 2,
        out_specs=WHOLE,
        out_shape=jax.ShapeDtypeStruct(even.shape, BF16),
        cost_estimate=cost(even.size, 4 * even.size),
        compiler_params=SMALL,
        name="across",
    )(even, odd)


def factor_kernel(pair_scale, mask, out):
    row, col = lax.axis_index("row"), lax.axis_index("col")
    rows, cols = lax.axis_size("row"), lax.axis_size("col")
    for d in range(8):
        k = d + d // 4
        r, c = row + k // 3 - 1, col + k % 3 - 1
        inside = (r >= 0) & (r < rows) & (c >= 0) & (c < cols)
        factor = jnp.where(inside, mask[0, d].astype(F32) * pair_scale, 0.0)
        out[d] = jnp.full(out.shape[1:], factor, F32)


def factor_call(mask, basis, pair_scale):
    return pl.pallas_call(
        functools.partial(factor_kernel, pair_scale),
        in_specs=[SMEM],
        out_specs=WHOLE,
        out_shape=jax.ShapeDtypeStruct((8, 8, basis), F32),
        cost_estimate=cost(64, 64 * basis),
        compiler_params=SMALL,
        name="factor",
    )(mask)


def finish_kernel(scales, factors, full_mine, full_theirs, *refs):
    self_scale, full_scale = scales
    ins, (self_out, pair_out, full_out) = refs[:-3], refs[-3:]
    basis = self_out.shape[1]
    row, col = lax.axis_index("row"), lax.axis_index("col")
    even_right = 1 - col % 2

    def put(down, right, value):
        d = (down + 1) * 3 + right + 1
        d = d - (d > 4).astype(jnp.int32)
        pair_out[d] = value * factors[d, 0:1, :]

    to_even, to_odd = 2 * even_right - 1, 1 - 2 * even_right
    full_out[...] = (full_mine[...] + full_theirs[...]) * full_scale
    if len(ins) == 5:
        for d in range(3):
            pair_out[jnp.where(row % 2 == 0, d, 5 + d)] = jnp.zeros_like(full_mine)
    for shift in range(len(ins) // 5):
        stay, even, odd, early, late = ins[5 * shift : 5 * shift + 5]
        down = 2 * (row % 2 == shift).astype(jnp.int32) - 1
        keep = [stay[0] + even[0].astype(F32), stay[1] + odd[0].astype(F32), stay[2]]
        got = [early[k].astype(F32) + late[k].astype(F32) for k in range(2)] + [early[2].astype(F32)]
        own = [keep[k][:, :basis] + got[k][:, basis:] for k in range(3)]
        other = [keep[k][:, basis:] + got[k][:, :basis] for k in range(3)]
        put(down, to_even, other[0])
        put(down, to_odd, other[1])
        put(down, 0, other[2])
        if shift == 0:
            put(0, to_even, own[0])
            put(0, to_odd, own[1])
            self_out[...] = own[2] * self_scale


def finish_call(factors, full, results, scales):
    args = [factors, *full, *(a for result in results for a in result)]
    half, basis = full[0].shape
    side = jax.ShapeDtypeStruct((half, basis), F32)
    return pl.pallas_call(
        functools.partial(finish_kernel, scales),
        in_specs=[WHOLE] * len(args),
        out_specs=[WHOLE] * 3,
        out_shape=[side, jax.ShapeDtypeStruct((8, half, basis), F32), side],
        cost_estimate=cost(20 * half * basis, 80 * half * basis),
        compiler_params=SMALL,
        name="finish",
    )(*args)


def in_hbm(value):
    return pltpu.with_memory_space_constraint(value, pltpu.HBM)


def row_pairs(rows, shift):
    first = [(i, i + 1) for i in range(shift, rows - 1, 2)]
    return first + [(j, i) for i, j in first]


def beside(value, first):
    cols, sides = lax.axis_size("col"), lax.axis_size("aux")
    pairs = []
    for c in range(cols):
        other = c ^ 1 if first == 0 else ((c - 1) ^ 1) + 1
        for a in range(sides):
            inside = 0 <= other < cols
            pairs.append((c * sides + a, other * sides + a if inside else c * sides + (a + 1) % sides))
    return lax.ppermute(value, ("col", "aux"), pairs)


def local(coef_three, orbitals, density, pair_mask, *, full_q):
    _, _, q, width = coef_three.shape
    occupied, basis = orbitals.shape[2:]
    rows = lax.axis_size("row")
    coef = in_hbm(coef_three.reshape(q, width))
    quarter = occupied // 4
    sizes = [quarter - quarter // 5 - 3 * quarter // 10, 3 * quarter // 10, quarter // 5]
    parts = 2
    orb, dens = in_hbm(orbitals[0, 0]), density[0, 0]
    ke0, ko0, se0, so0, kept0 = half_call(coef, orb, 0, parts, [quarter] * 4)
    ke1, ko1, *pieces1, kept1 = half_call(coef, orb, 1, parts, [quarter] * 2 + sizes * 2)
    full = full_call(kept1, dens, full_call(kept0, dens, ()))
    swap_sides = [(0, 1), (1, 0)]
    full = (full[0], lax.ppermute(full[1], "aux", swap_sides))
    near0 = (ke0, ko0, beside(ke0, 0), beside(ko0, 1))
    near1 = (ke1, ko1, beside(ke1, 0), beside(ko1, 1))
    plan, start = [(0, near0, se0, so0)], 0
    for k, size in enumerate(sizes):
        plan.append((start, near1, pieces1[k], pieces1[len(sizes) + k]))
        start += size * (q // parts)
    results = []
    for shift in range(min(2, rows - 1)):
        swap = row_pairs(rows, shift)
        pieces = []
        for _, _, send_e, send_o in plan:
            y_e = lax.ppermute(send_e, "row", swap)
            y_o = lax.ppermute(send_o, "row", swap)
            pieces.append((y_e, y_o, beside(y_e, 0), beside(y_o, 1)))
        sums = ()
        for k, (start, near, _, _) in enumerate(plan):
            last = k == len(plan) - 1
            sums = meet_call(start, near, pieces[k], sums, last)
        mine, theirs = sums
        stay, even, odd, send = joined_call(mine, lax.ppermute(theirs, "aux", swap_sides))
        even, odd = beside(even, 0), beside(odd, 1)
        early = lax.ppermute(send, "row", swap)
        late = lax.ppermute(across_call(even, odd), "row", swap)
        results.append((stay, even, odd, early, late))
    factors = factor_call(pair_mask[0], basis, 1.0 / (full_q * occupied) ** 0.5)
    scales = (1.0 / (full_q * occupied), 1.0 / (full_q * basis) ** 0.5)
    exch_self, pair, exch_full = finish_call(factors, full, results, scales)
    return exch_self[None, None], pair[None, None], exch_full[None, None]


def solution(mesh):
    in_specs = (
        P(("sys", "row"), "col", "aux", None),
        P(("sys", "row"), "col", None, None),
        P(("sys", "row"), "col", None, None),
        P(("sys", "row"), "col", None),
    )
    out_specs = (
        P(("sys", "row"), "col", "aux", None),
        P(("sys", "row"), "col", None, "aux", None),
        P(("sys", "row"), "col", "aux", None),
    )

    def whole(coef_three, orbitals, density, pair_mask):
        return jax.shard_map(
            functools.partial(local, full_q=coef_three.shape[2]),
            mesh=mesh,
            in_specs=in_specs,
            out_specs=out_specs,
            check_vma=False,
        )(coef_three, orbitals, density, pair_mask)

    return whole
```

```python
import functools

import jax
import jax.numpy as jnp
from jax import lax
from jax.experimental import pallas as pl
from jax.experimental.pallas import tpu as pltpu
from jax.sharding import PartitionSpec as P


LANES = 128
NT = (((1,), (1,)), ((), ()))
HBM = pl.BlockSpec(memory_space=pltpu.HBM)
WHOLE = pl.BlockSpec(memory_space=pltpu.VMEM)
SMEM = pl.BlockSpec(memory_space=pltpu.SMEM)
F32 = jnp.float32
BF16 = jnp.bfloat16
BATCH = 4
MIB = 2**20
SMALL = pltpu.CompilerParams(vmem_limit_bytes=12 * MIB)


def cost(flops, size):
    return pl.CostEstimate(flops=int(flops), bytes_accessed=int(size), transcendentals=0)


def odd_pitch(rows):
    return rows + 8 * (1 - (rows // 8) % 2)


def block(i, size):
    return pl.ds(pl.multiple_of(i * size, size), size)


def put_slabs(scratch, group, left, kept, i):
    height, (slabs, rows, lanes) = left.shape[0], scratch.shape
    pitch, q = rows // group, slabs * lanes
    for j in range(0, group, BATCH):
        first = pl.multiple_of((i * group + j) * q, BATCH * q)
        value = nt(left, kept[pl.ds(first, BATCH * q), :])
        for k in range(BATCH * slabs):
            at = (j + k // slabs) * pitch
            scratch[k % slabs, at : at + height, :] = value[:, k * lanes : (k + 1) * lanes]
    return pitch


def half_kernel(part, group, counts, coef, orb, *refs):
    outs, (kept, scratch, orb_ref, arrived) = refs[:-4], refs[-4:]
    occupied, basis = orb.shape
    slabs, _, lanes = scratch.shape
    q = slabs * lanes
    steps = basis // group
    quarter = occupied // 4
    flip_row = lax.axis_index("row") % 2
    flip_col = lax.axis_index("col") % 2
    copy = pltpu.make_async_copy(orb, orb_ref, arrived.at[steps])
    copy.start()

    @pl.loop(0, steps)
    def _(i):
        for j in range(group):
            k = i * group + j
            pltpu.make_async_copy(
                coef.at[part * q : (part + 1) * q, block(k, basis)], kept.at[block(k, q), :], arrived.at[i]
            ).start()

    copy.wait()
    orb = orb_ref[...]

    @pl.loop(0, steps)
    def _(i):
        here = kept.at[block(i, group * q), :]
        pltpu.make_async_copy(here, here, arrived.at[i]).wait()
        pitch = put_slabs(scratch, group, orb, kept, i)
        o = 0
        for out, count in zip(outs, counts):
            for k in range(count):
                send, turn = o // (2 * quarter), o // quarter % 2
                away = flip_row if send == 0 else 1 - flip_row
                over = 1 - flip_col if turn == 0 else flip_col
                row = o % quarter + 2 * quarter * away + quarter * over
                for h in range(slabs):
                    at = (k * slabs + h) * lanes
                    out[block(i, group), at : at + lanes] = scratch[h, pl.ds(row, group, stride=pitch), :].astype(BF16)
                o += 1


def half_call(coef, orb, part, parts, counts, group=32):
    q, width = coef.shape
    q //= parts
    occupied, basis = orb.shape
    shapes = [(basis, n * q) for n in counts] + [(basis * q, basis)]
    return pl.pallas_call(
        functools.partial(half_kernel, part, group, counts),
        in_specs=[HBM, HBM],
        out_specs=[WHOLE] * len(shapes),
        out_shape=[jax.ShapeDtypeStruct(shape, BF16) for shape in shapes],
        scratch_shapes=[
            pltpu.VMEM((q // LANES, group * odd_pitch(occupied), LANES), F32),
            pltpu.VMEM(orb.shape, BF16),
            pltpu.SemaphoreType.DMA((basis // group + 1,)),
        ],
        cost_estimate=cost(2 * q * width * occupied, 2 * q * width + 2 * occupied * basis * q),
        compiler_params=pltpu.CompilerParams(vmem_limit_bytes=16 * MIB),
    )(coef, orb)


def full_kernel(group, kept, dens_ref, *refs):
    before, outs, (turned, scratch) = refs[:-4], refs[-4:-2], refs[-2:]
    basis = dens_ref.shape[0]
    slabs, _, lanes = scratch.shape
    q = slabs * lanes
    dens = dens_ref[...].T

    @pl.loop(0, basis // group)
    def _(i):
        pitch = put_slabs(scratch, group, dens, kept, i)
        for s in range(basis):
            for h in range(slabs):
                at = s * q + h * lanes
                turned[block(i, group), at : at + lanes] = scratch[h, pl.ds(s, group, stride=pitch), :].astype(BF16)

    total = before[0][...] + before[1][...] if before else jnp.zeros((basis, basis), F32)
    span = basis // 2 * q
    for first in range(0, basis * q, span):
        total += jnp.dot(turned[:, first : first + span], kept[first : first + span, :], preferred_element_type=F32)
    half = basis // 2
    side = lax.axis_index("aux")
    if before:
        scratch[0, :basis, :] = total
        outs[0][...] = scratch[0, block(side, half), :]
        outs[1][...] = scratch[0, block(1 - side, half), :]
    else:
        outs[0][...] = total
        outs[1][...] = jnp.zeros_like(outs[1])


def full_call(kept, dens, before, group=64):
    basis = dens.shape[0]
    q = kept.shape[0] // basis
    height = basis // 2 if before else basis
    out = jax.ShapeDtypeStruct((height, basis), F32)
    args = [kept, dens, *before]
    return pl.pallas_call(
        functools.partial(full_kernel, group),
        in_specs=[WHOLE] * len(args),
        out_specs=[WHOLE] * 2,
        out_shape=[out, out],
        scratch_shapes=[
            pltpu.VMEM((basis, basis * q), BF16),
            pltpu.VMEM((q // LANES, group * odd_pitch(basis), LANES), F32),
        ],
        compiler_params=pltpu.CompilerParams(vmem_limit_bytes=16 * MIB),
        cost_estimate=cost(4 * q * basis**3, 2 * q * basis**2),
    )(*args)


def nt(left, right):
    return lax.dot_general(left, right, NT, preferred_element_type=F32)


def meet(start, x_e, x_o, far_e, far_o, y_e, y_o, farther_e, farther_o):
    here = slice(start, start + y_e.shape[1])
    near_e = jnp.concatenate([x_e[:, here], y_e[...]])
    near_o = jnp.concatenate([x_o[:, here], y_o[...]])
    even = nt(near_o, jnp.concatenate([far_e[:, here], farther_e[...]]))
    odd = nt(near_e, jnp.concatenate([far_o[:, here], farther_o[...]]))
    return even, odd, nt(near_e, near_e) + nt(near_o, near_o)


def meet_kernel(start, *refs):
    before, outs = refs[8:-3], refs[-3:]
    for k, value in enumerate(meet(start, *refs[:8])):
        outs[k][...] = value + before[k][...] if before else value


def last_kernel(start, *refs):
    before, (mine, theirs, lines) = refs[8:-3], refs[-3:]
    basis = mine.shape[2] // 2
    half = basis // 2
    sums = list(meet(start, *refs[:8]))
    for k, part in enumerate(before):
        sums[k] += part[...]
    for k in range(3):
        lines[k] = sums[k][:basis]
        lines[3 + k] = sums[k][basis:]
    for k in range(2):
        turned = sums[k].T
        lines[6 + 2 * k] = turned[:basis]
        lines[7 + 2 * k] = turned[basis:]
    side = lax.axis_index("aux")
    mine[...] = lines[:, pl.ds(pl.multiple_of(side * half, half), half), :]
    theirs[...] = lines[:, pl.ds(pl.multiple_of((1 - side) * half, half), half), :].astype(BF16)


def meet_call(start, xs, ys, before, last):
    basis, width = ys[0].shape
    two = jax.ShapeDtypeStruct((2 * basis, 2 * basis), F32)
    out = jax.ShapeDtypeStruct((10, basis // 2, 2 * basis), F32)
    args = [*xs, *ys, *before]
    shapes = [out, jax.ShapeDtypeStruct(out.shape, BF16)] if last else [two, two, two]
    return pl.pallas_call(
        functools.partial(last_kernel if last else meet_kernel, start),
        in_specs=[WHOLE] * len(args),
        out_specs=[WHOLE] * len(shapes),
        out_shape=shapes,
        scratch_shapes=[pltpu.VMEM((10, basis, 2 * basis), F32)] if last else [],
        cost_estimate=cost(24 * basis * basis * width, 16 * basis * width),
        compiler_params=SMALL,
    )(*args)


def joined_kernel(mine, theirs, stay, rows, *onward):
    stay[...] = mine[0:3] + theirs[0:3].astype(F32)
    rows[...] = (mine[3:6] + theirs[3:6].astype(F32)).astype(BF16)
    for k, out in enumerate(onward):
        out[...] = (mine[6 + k] + theirs[6 + k].astype(F32)).astype(BF16)


def joined_call(mine, theirs):
    _, half, two = mine.shape
    line = jax.ShapeDtypeStruct((half, two), BF16)
    shapes = [jax.ShapeDtypeStruct((3, half, two), F32), jax.ShapeDtypeStruct((3, half, two), BF16)] + [line] * 4
    return pl.pallas_call(
        joined_kernel,
        in_specs=[WHOLE] * 2,
        out_specs=[WHOLE] * 6,
        out_shape=shapes,
        cost_estimate=cost(mine.size, 12 * mine.size),
        compiler_params=SMALL,
    )(mine, theirs)


def factor_kernel(pair_scale, mask, out):
    row, col = lax.axis_index("row"), lax.axis_index("col")
    rows, cols = lax.axis_size("row"), lax.axis_size("col")
    for d in range(8):
        k = d + d // 4
        r, c = row + k // 3 - 1, col + k % 3 - 1
        inside = (r >= 0) & (r < rows) & (c >= 0) & (c < cols)
        factor = jnp.where(inside, mask[0, d].astype(F32) * pair_scale, 0.0)
        out[d] = jnp.full(out.shape[1:], factor, F32)


def factor_call(mask, basis, pair_scale):
    return pl.pallas_call(
        functools.partial(factor_kernel, pair_scale),
        in_specs=[SMEM],
        out_specs=WHOLE,
        out_shape=jax.ShapeDtypeStruct((8, 8, basis), F32),
        cost_estimate=cost(64, 64 * basis),
        compiler_params=SMALL,
        name="factor",
    )(mask)


def finish_kernel(scales, factors, full_mine, full_theirs, *refs):
    self_scale, full_scale = scales
    ins, (self_out, pair_out, full_out) = refs[:-3], refs[-3:]
    basis = self_out.shape[1]
    row, col = lax.axis_index("row"), lax.axis_index("col")
    even_right = 1 - col % 2

    def put(down, right, value):
        d = (down + 1) * 3 + right + 1
        d = d - (d > 4).astype(jnp.int32)
        pair_out[d] = value * factors[d, 0:1, :]

    to_even, to_odd = 2 * even_right - 1, 1 - 2 * even_right
    full_out[...] = (full_mine[...] + full_theirs[...]) * full_scale
    if len(ins) == 6:
        for d in range(3):
            pair_out[jnp.where(row % 2 == 0, d, 5 + d)] = jnp.zeros_like(full_mine)
    for shift in range(len(ins) // 6):
        stay, even, odd, rows, even_far, odd_far = ins[6 * shift : 6 * shift + 6]
        down = 2 * (row % 2 == shift).astype(jnp.int32) - 1
        keep = [stay[0] + even[...].astype(F32), stay[1] + odd[...].astype(F32), stay[2]]
        got = [rows[k].astype(F32) for k in range(3)]
        got[0] += even_far[...].astype(F32)
        got[1] += odd_far[...].astype(F32)
        own = [keep[k][:, :basis] + got[k][:, basis:] for k in range(3)]
        other = [keep[k][:, basis:] + got[k][:, :basis] for k in range(3)]
        put(down, to_even, other[0])
        put(down, to_odd, other[1])
        put(down, 0, other[2])
        if shift == 0:
            put(0, to_even, own[0])
            put(0, to_odd, own[1])
            self_out[...] = own[2] * self_scale


def finish_call(factors, full, results, scales):
    args = [factors, *full, *(a for result in results for a in result)]
    half, basis = full[0].shape
    side = jax.ShapeDtypeStruct((half, basis), F32)
    return pl.pallas_call(
        functools.partial(finish_kernel, scales),
        in_specs=[WHOLE] * len(args),
        out_specs=[WHOLE] * 3,
        out_shape=[side, jax.ShapeDtypeStruct((8, half, basis), F32), side],
        cost_estimate=cost(20 * half * basis, 80 * half * basis),
        compiler_params=SMALL,
        name="finish",
    )(*args)


def in_hbm(value):
    return pltpu.with_memory_space_constraint(value, pltpu.HBM)


def row_pairs(rows, shift):
    first = [(i, i + 1) for i in range(shift, rows - 1, 2)]
    return first + [(j, i) for i, j in first]


def beside(value, first, swap=None):
    cols, sides = lax.axis_size("col"), lax.axis_size("aux")
    near = []
    for c in range(cols):
        other = c ^ 1 if first == 0 else ((c - 1) ^ 1) + 1
        for a in range(sides):
            inside = 0 <= other < cols
            near.append((c * sides + a, other * sides + a if inside else c * sides + (a + 1) % sides))
    if swap is None:
        return lax.ppermute(value, ("col", "aux"), near)
    size = cols * sides
    far = [(r * size + source, t * size + target) for r, t in swap for source, target in near]
    return lax.ppermute(value, ("row", "col", "aux"), far)


def local(coef_three, orbitals, density, pair_mask, *, full_q):
    _, _, q, width = coef_three.shape
    occupied, basis = orbitals.shape[2:]
    rows = lax.axis_size("row")
    coef = in_hbm(coef_three.reshape(q, width))
    quarter = occupied // 4
    small = max(1, quarter // 5)
    big = quarter - small
    parts = 2
    orb, dens = in_hbm(orbitals[0, 0]), density[0, 0]
    ke0, ko0, se0, so0, kept0 = half_call(coef, orb, 0, parts, [quarter] * 4)
    ke1, ko1, se1, se2, so1, so2, kept1 = half_call(
        coef, orb, 1, parts, [quarter, quarter, big, small, big, small]
    )
    full = full_call(kept1, dens, full_call(kept0, dens, ()))
    swap_sides = [(0, 1), (1, 0)]
    full = (full[0], lax.ppermute(full[1], "aux", swap_sides))
    near0 = (ke0, ko0, beside(ke0, 0), beside(ko0, 1))
    near1 = (ke1, ko1, beside(ke1, 0), beside(ko1, 1))
    plan = ((0, near0, se0, so0), (0, near1, se1, so1), (big * (q // parts), near1, se2, so2))
    results = []
    for shift in range(min(2, rows - 1)):
        swap = row_pairs(rows, shift)
        pieces = []
        for _, _, send_e, send_o in plan:
            y_e = lax.ppermute(send_e, "row", swap)
            y_o = lax.ppermute(send_o, "row", swap)
            pieces.append((y_e, y_o, beside(y_e, 0), beside(y_o, 1)))
        sums = ()
        for k, (start, near, _, _) in enumerate(plan):
            last = k == len(plan) - 1
            sums = meet_call(start, near, pieces[k], sums, last)
        mine, theirs = sums
        theirs = lax.ppermute(theirs, "aux", swap_sides)
        stay, own_rows, even, even_far, odd, odd_far = joined_call(mine, theirs)
        results.append(
            (
                stay,
                beside(even, 0),
                beside(odd, 1),
                lax.ppermute(own_rows, "row", swap),
                beside(even_far, 0, swap),
                beside(odd_far, 1, swap),
            )
        )
    factors = factor_call(pair_mask[0], basis, 1.0 / (full_q * occupied) ** 0.5)
    scales = (1.0 / (full_q * occupied), 1.0 / (full_q * basis) ** 0.5)
    exch_self, pair, exch_full = finish_call(factors, full, results, scales)
    return exch_self[None, None], pair[None, None], exch_full[None, None]


def solution(mesh):
    in_specs = (
        P(("sys", "row"), "col", "aux", None),
        P(("sys", "row"), "col", None, None),
        P(("sys", "row"), "col", None, None),
        P(("sys", "row"), "col", None),
    )
    out_specs = (
        P(("sys", "row"), "col", "aux", None),
        P(("sys", "row"), "col", None, "aux", None),
        P(("sys", "row"), "col", "aux", None),
    )

    def whole(coef_three, orbitals, density, pair_mask):
        return jax.shard_map(
            functools.partial(local, full_q=coef_three.shape[2]),
            mesh=mesh,
            in_specs=in_specs,
            out_specs=out_specs,
            check_vma=False,
        )(coef_three, orbitals, density, pair_mask)

    return whole
```

```python
import functools

import jax
import jax.numpy as jnp
from jax import lax
from jax.experimental import pallas as pl
from jax.experimental.pallas import tpu as pltpu
from jax.sharding import PartitionSpec as P


LANES = 128
NT = (((1,), (1,)), ((), ()))
HBM = pl.BlockSpec(memory_space=pltpu.HBM)
WHOLE = pl.BlockSpec(memory_space=pltpu.VMEM)
SMEM = pl.BlockSpec(memory_space=pltpu.SMEM)
F32 = jnp.float32
BF16 = jnp.bfloat16
BATCH = 4
MIB = 2**20
SMALL = pltpu.CompilerParams(vmem_limit_bytes=12 * MIB)


def cost(flops, size):
    return pl.CostEstimate(flops=int(flops), bytes_accessed=int(size), transcendentals=0)


def odd_pitch(rows):
    return rows + 8 * (1 - (rows // 8) % 2)


def block(i, size):
    return pl.ds(pl.multiple_of(i * size, size), size)


def put_slabs(scratch, group, left, kept, i):
    height, (slabs, rows, lanes) = left.shape[0], scratch.shape
    pitch, q = rows // group, slabs * lanes
    for j in range(0, group, BATCH):
        first = pl.multiple_of((i * group + j) * q, BATCH * q)
        value = nt(left, kept[pl.ds(first, BATCH * q), :])
        for k in range(BATCH * slabs):
            at = (j + k // slabs) * pitch
            scratch[k % slabs, at : at + height, :] = value[:, k * lanes : (k + 1) * lanes]
    return pitch


def half_kernel(part, group, counts, coef, orb, *refs):
    outs, (kept, scratch, orb_ref, arrived) = refs[:-4], refs[-4:]
    occupied, basis = orb.shape
    slabs, _, lanes = scratch.shape
    q = slabs * lanes
    steps = basis // group
    quarter = occupied // 4
    flip_row = lax.axis_index("row") % 2
    flip_col = lax.axis_index("col") % 2
    copy = pltpu.make_async_copy(orb, orb_ref, arrived.at[steps])
    copy.start()

    @pl.loop(0, steps)
    def _(i):
        for j in range(group):
            k = i * group + j
            pltpu.make_async_copy(
                coef.at[part * q : (part + 1) * q, block(k, basis)], kept.at[block(k, q), :], arrived.at[i]
            ).start()

    copy.wait()
    orb = orb_ref[...]

    @pl.loop(0, steps)
    def _(i):
        here = kept.at[block(i, group * q), :]
        pltpu.make_async_copy(here, here, arrived.at[i]).wait()
        pitch = put_slabs(scratch, group, orb, kept, i)
        o = 0
        for out, count in zip(outs, counts):
            for k in range(count):
                send, turn = o // (2 * quarter), o // quarter % 2
                away = flip_row if send == 0 else 1 - flip_row
                over = 1 - flip_col if turn == 0 else flip_col
                row = o % quarter + 2 * quarter * away + quarter * over
                for h in range(slabs):
                    at = (k * slabs + h) * lanes
                    out[block(i, group), at : at + lanes] = scratch[h, pl.ds(row, group, stride=pitch), :].astype(BF16)
                o += 1


def half_call(coef, orb, part, parts, counts, group=32):
    q, width = coef.shape
    q //= parts
    occupied, basis = orb.shape
    shapes = [(basis, n * q) for n in counts] + [(basis * q, basis)]
    return pl.pallas_call(
        functools.partial(half_kernel, part, group, counts),
        in_specs=[HBM, HBM],
        out_specs=[WHOLE] * len(shapes),
        out_shape=[jax.ShapeDtypeStruct(shape, BF16) for shape in shapes],
        scratch_shapes=[
            pltpu.VMEM((q // LANES, group * odd_pitch(occupied), LANES), F32),
            pltpu.VMEM(orb.shape, BF16),
            pltpu.SemaphoreType.DMA((basis // group + 1,)),
        ],
        cost_estimate=cost(2 * q * width * occupied, 2 * q * width + 2 * occupied * basis * q),
        compiler_params=pltpu.CompilerParams(vmem_limit_bytes=16 * MIB),
    )(coef, orb)


def full_kernel(group, kept, dens_ref, *refs):
    before, outs, (turned, scratch) = refs[:-4], refs[-4:-2], refs[-2:]
    basis = dens_ref.shape[0]
    slabs, _, lanes = scratch.shape
    q = slabs * lanes
    dens = dens_ref[...].T

    @pl.loop(0, basis // group)
    def _(i):
        pitch = put_slabs(scratch, group, dens, kept, i)
        for s in range(basis):
            for h in range(slabs):
                at = s * q + h * lanes
                turned[block(i, group), at : at + lanes] = scratch[h, pl.ds(s, group, stride=pitch), :].astype(BF16)

    total = before[0][...] + before[1][...] if before else jnp.zeros((basis, basis), F32)
    span = basis // 2 * q
    for first in range(0, basis * q, span):
        total += jnp.dot(turned[:, first : first + span], kept[first : first + span, :], preferred_element_type=F32)
    half = basis // 2
    side = lax.axis_index("aux")
    if before:
        scratch[0, :basis, :] = total
        outs[0][...] = scratch[0, block(side, half), :]
        outs[1][...] = scratch[0, block(1 - side, half), :]
    else:
        outs[0][...] = total
        outs[1][...] = jnp.zeros_like(outs[1])


def full_call(kept, dens, before, group=64):
    basis = dens.shape[0]
    q = kept.shape[0] // basis
    height = basis // 2 if before else basis
    out = jax.ShapeDtypeStruct((height, basis), F32)
    args = [kept, dens, *before]
    return pl.pallas_call(
        functools.partial(full_kernel, group),
        in_specs=[WHOLE] * len(args),
        out_specs=[WHOLE] * 2,
        out_shape=[out, out],
        scratch_shapes=[
            pltpu.VMEM((basis, basis * q), BF16),
            pltpu.VMEM((q // LANES, group * odd_pitch(basis), LANES), F32),
        ],
        compiler_params=pltpu.CompilerParams(vmem_limit_bytes=16 * MIB),
        cost_estimate=cost(4 * q * basis**3, 2 * q * basis**2),
    )(*args)


def nt(left, right):
    return lax.dot_general(left, right, NT, preferred_element_type=F32)


def over(upper, lower):
    return jnp.concatenate([upper, lower])


def wide(refs):
    return jnp.concatenate([r[...] for r in refs], axis=1) if len(refs) > 1 else refs[0][...]


def sums_of(span_e, span_o, square, x_e, x_o, far_e, far_o, farther_e, farther_o, y_e, y_o):
    near_e, near_o = over(x_e[...], wide(y_e)), over(x_o[...], wide(y_o))
    even = nt(near_o[:, span_e], over(far_e[:, span_e], farther_e[...]))
    odd = nt(near_e[:, span_o], over(far_o[:, span_o], farther_o[...]))
    return even, odd, nt(near_e, near_e) + nt(near_o, near_o) if square else 0.0


def meet_kernel(spans, count, *refs):
    fixed, y_e, y_o = refs[:6], refs[6 : 6 + count], refs[6 + count : 6 + 2 * count]
    before, outs = refs[6 + 2 * count : -3], refs[-3:]
    for k, value in enumerate(sums_of(*spans, True, *fixed, y_e, y_o)):
        outs[k][...] = value + before[k][...] if before else value


def last_kernel(spans, count, *refs):
    fixed, y_e, y_o = refs[:6], refs[6 : 6 + count], refs[6 + count : 6 + 2 * count]
    before, (mine, theirs, lines) = refs[6 + 2 * count : -3], refs[-3:]
    basis = mine.shape[2] // 2
    half = basis // 2
    sums = [part[...] + value for part, value in zip(before, sums_of(*spans, False, *fixed, y_e, y_o))]
    for k in range(3):
        lines[k] = sums[k][:basis]
        lines[3 + k] = sums[k][basis:]
    for k in range(2):
        turned = sums[k].T
        lines[6 + 2 * k] = turned[:basis]
        lines[7 + 2 * k] = turned[basis:]
    side = lax.axis_index("aux")
    mine[...] = lines[:, block(side, half), :]
    theirs[...] = lines[:, block(1 - side, half), :].astype(BF16)


def meet_call(spans, near, relays, y_e, y_o, before, last):
    basis, width = near[0].shape
    two = jax.ShapeDtypeStruct((2 * basis, 2 * basis), F32)
    out = jax.ShapeDtypeStruct((10, basis // 2, 2 * basis), F32)
    args = [*near, *relays, *y_e, *y_o, *before]
    shapes = [out, jax.ShapeDtypeStruct(out.shape, BF16)] if last else [two, two, two]
    return pl.pallas_call(
        functools.partial(last_kernel if last else meet_kernel, spans, len(y_e)),
        in_specs=[WHOLE] * len(args),
        out_specs=[WHOLE] * len(shapes),
        out_shape=shapes,
        scratch_shapes=[pltpu.VMEM((10, basis, 2 * basis), F32)] if last else [],
        cost_estimate=cost(24 * basis * basis * width, 16 * basis * width),
        compiler_params=SMALL,
    )(*args)


def joined_kernel(mine, theirs, stay, rows, *onward):
    stay[...] = mine[0:3] + theirs[0:3].astype(F32)
    rows[...] = (mine[3:6] + theirs[3:6].astype(F32)).astype(BF16)
    for k, out in enumerate(onward):
        out[...] = (mine[6 + k] + theirs[6 + k].astype(F32)).astype(BF16)


def joined_call(mine, theirs):
    _, half, two = mine.shape
    line = jax.ShapeDtypeStruct((half, two), BF16)
    shapes = [jax.ShapeDtypeStruct((3, half, two), F32), jax.ShapeDtypeStruct((3, half, two), BF16)] + [line] * 4
    return pl.pallas_call(
        joined_kernel,
        in_specs=[WHOLE] * 2,
        out_specs=[WHOLE] * 6,
        out_shape=shapes,
        cost_estimate=cost(mine.size, 12 * mine.size),
        compiler_params=SMALL,
    )(mine, theirs)


def factor_kernel(pair_scale, mask, out):
    row, col = lax.axis_index("row"), lax.axis_index("col")
    rows, cols = lax.axis_size("row"), lax.axis_size("col")
    for d in range(8):
        k = d + d // 4
        r, c = row + k // 3 - 1, col + k % 3 - 1
        inside = (r >= 0) & (r < rows) & (c >= 0) & (c < cols)
        factor = jnp.where(inside, mask[0, d].astype(F32) * pair_scale, 0.0)
        out[d] = jnp.full(out.shape[1:], factor, F32)


def factor_call(mask, basis, pair_scale):
    return pl.pallas_call(
        functools.partial(factor_kernel, pair_scale),
        in_specs=[SMEM],
        out_specs=WHOLE,
        out_shape=jax.ShapeDtypeStruct((8, 8, basis), F32),
        cost_estimate=cost(64, 64 * basis),
        compiler_params=SMALL,
        name="factor",
    )(mask)


def finish_kernel(scales, factors, full_mine, full_theirs, *refs):
    self_scale, full_scale = scales
    ins, (self_out, pair_out, full_out) = refs[:-3], refs[-3:]
    basis = self_out.shape[1]
    row, col = lax.axis_index("row"), lax.axis_index("col")
    even_right = 1 - col % 2

    def put(down, right, value):
        d = (down + 1) * 3 + right + 1
        d = d - (d > 4).astype(jnp.int32)
        pair_out[d] = value * factors[d, 0:1, :]

    to_even, to_odd = 2 * even_right - 1, 1 - 2 * even_right
    full_out[...] = (full_mine[...] + full_theirs[...]) * full_scale
    if len(ins) == 6:
        for d in range(3):
            pair_out[jnp.where(row % 2 == 0, d, 5 + d)] = jnp.zeros_like(full_mine)
    for shift in range(len(ins) // 6):
        stay, even, odd, rows, even_far, odd_far = ins[6 * shift : 6 * shift + 6]
        down = 2 * (row % 2 == shift).astype(jnp.int32) - 1
        keep = [stay[0] + even[...].astype(F32), stay[1] + odd[...].astype(F32), stay[2]]
        got = [rows[k].astype(F32) for k in range(3)]
        got[0] += even_far[...].astype(F32)
        got[1] += odd_far[...].astype(F32)
        own = [keep[k][:, :basis] + got[k][:, basis:] for k in range(3)]
        other = [keep[k][:, basis:] + got[k][:, :basis] for k in range(3)]
        put(down, to_even, other[0])
        put(down, to_odd, other[1])
        put(down, 0, other[2])
        if shift == 0:
            put(0, to_even, own[0])
            put(0, to_odd, own[1])
            self_out[...] = own[2] * self_scale


def finish_call(factors, full, results, scales):
    args = [factors, *full, *(a for result in results for a in result)]
    half, basis = full[0].shape
    side = jax.ShapeDtypeStruct((half, basis), F32)
    return pl.pallas_call(
        functools.partial(finish_kernel, scales),
        in_specs=[WHOLE] * len(args),
        out_specs=[WHOLE] * 3,
        out_shape=[side, jax.ShapeDtypeStruct((8, half, basis), F32), side],
        cost_estimate=cost(20 * half * basis, 80 * half * basis),
        compiler_params=SMALL,
        name="finish",
    )(*args)


def in_hbm(value):
    return pltpu.with_memory_space_constraint(value, pltpu.HBM)


def row_pairs(rows, shift):
    first = [(i, i + 1) for i in range(shift, rows - 1, 2)]
    return first + [(j, i) for i, j in first]


def beside(value, first, swap=None):
    cols, sides = lax.axis_size("col"), lax.axis_size("aux")
    near = []
    for c in range(cols):
        other = c ^ 1 if first == 0 else ((c - 1) ^ 1) + 1
        for a in range(sides):
            inside = 0 <= other < cols
            near.append((c * sides + a, other * sides + a if inside else c * sides + (a + 1) % sides))
    if swap is None:
        return lax.ppermute(value, ("col", "aux"), near)
    size = cols * sides
    far = [(r * size + source, t * size + target) for r, t in swap for source, target in near]
    return lax.ppermute(value, ("row", "col", "aux"), far)


def local(coef_three, orbitals, density, pair_mask, *, full_q):
    _, _, q, width = coef_three.shape
    occupied, basis = orbitals.shape[2:]
    rows = lax.axis_size("row")
    coef = in_hbm(coef_three.reshape(q, width))
    quarter = occupied // 4
    small_e, small_o = max(1, 3 * quarter // 10), max(1, 4 * quarter // 10)
    parts = 2
    orb, dens = in_hbm(orbitals[0, 0]), density[0, 0]
    ke0, ko0, se0, so0, kept0 = half_call(coef, orb, 0, parts, [quarter] * 4)
    counts = [quarter, quarter, quarter - small_e, small_e, quarter - small_o, small_o]
    ke1, ko1, se1, se2, so1, so2, kept1 = half_call(coef, orb, 1, parts, counts)
    full = full_call(kept1, dens, full_call(kept0, dens, ()))
    swap_sides = [(0, 1), (1, 0)]
    full = (full[0], lax.ppermute(full[1], "aux", swap_sides))
    near0 = (ke0, ko0, beside(ke0, 0), beside(ko0, 1))
    near1 = (ke1, ko1, beside(ke1, 0), beside(ko1, 1))
    whole = slice(0, ke0.shape[1])
    cut_e, cut_o = se1.shape[1], so1.shape[1]
    results = []
    for shift in range(min(2, rows - 1)):
        swap = row_pairs(rows, shift)
        y_e, y_o, g_e, g_o = [], [], [], []
        for k, (send_e, send_o) in enumerate(((se0, so0), (se1, so1), (se2, so2))):
            y_e.append(lax.ppermute(send_e, "row", swap))
            y_o.append(lax.ppermute(send_o, "row", swap))
            g_e.append(beside(y_e[k], 0))
            g_o.append(beside(y_o[k], 1))
        sums = meet_call((whole, whole), near0, (g_e[0], g_o[0]), y_e[:1], y_o[:1], (), False)
        spans = (slice(0, cut_e), slice(0, cut_o))
        sums = meet_call(spans, near1, (g_e[1], g_o[1]), y_e[1:], y_o[1:], sums, False)
        spans = (slice(cut_e, whole.stop), slice(cut_o, whole.stop))
        sums = meet_call(spans, near1, (g_e[2], g_o[2]), y_e[1:], y_o[1:], sums, True)
        mine, theirs = sums
        theirs = lax.ppermute(theirs, "aux", swap_sides)
        stay, own_rows, even, even_far, odd, odd_far = joined_call(mine, theirs)
        results.append(
            (
                stay,
                beside(even, 0),
                beside(odd, 1),
                lax.ppermute(own_rows, "row", swap),
                beside(even_far, 0, swap),
                beside(odd_far, 1, swap),
            )
        )
    factors = factor_call(pair_mask[0], basis, 1.0 / (full_q * occupied) ** 0.5)
    scales = (1.0 / (full_q * occupied), 1.0 / (full_q * basis) ** 0.5)
    exch_self, pair, exch_full = finish_call(factors, full, results, scales)
    return exch_self[None, None], pair[None, None], exch_full[None, None]


def solution(mesh):
    in_specs = (
        P(("sys", "row"), "col", "aux", None),
        P(("sys", "row"), "col", None, None),
        P(("sys", "row"), "col", None, None),
        P(("sys", "row"), "col", None),
    )
    out_specs = (
        P(("sys", "row"), "col", "aux", None),
        P(("sys", "row"), "col", None, "aux", None),
        P(("sys", "row"), "col", "aux", None),
    )

    def whole(coef_three, orbitals, density, pair_mask):
        return jax.shard_map(
            functools.partial(local, full_q=coef_three.shape[2]),
            mesh=mesh,
            in_specs=in_specs,
            out_specs=out_specs,
            check_vma=False,
        )(coef_three, orbitals, density, pair_mask)

    return whole
```
